256 devices in a mesh: dp: 16 (over z_hi, y), fsdp: 16 (over x, z_lo, core).
Axes of the slice: x: 4, y: 4, z: 8 (z_hi: 4, z_lo: 2; z = z_hi * 2 + z_lo), core: 2. Of those that a mesh axis runs over, the one named last changes fastest.
Arguments:
- features: bfloat16 [49152, 8192], P(('dp', 'fsdp')), may hold values from -6 to 6
- grad_out: bfloat16 [49152, 8192], P(('dp', 'fsdp')), may hold values from -6 to 6
- weight_tiles: bfloat16 [256, 128, 128], P('fsdp'), may hold values from -0.25 to 0.25
- tile_row: int32 [256], replicated, may hold values from 0 to 63, as said below
- tile_column: int32 [256], replicated, may hold values from 0 to 63, as said below
Outputs:
- grad_features: bfloat16 [49152, 8192], P(('dp', 'fsdp'))
- tile_update: float32 [256, 128, 128], P('fsdp')
The draws below stay inside these ranges and needn't reach their ends.
Inputs may be any that keep to these rules, and one draw needn't show every extreme that they name: `tile_row`: every tile-row holds exactly 4 stored tiles; the tile-columns of tile-row i are i XOR s for the four values s in (0, 2^a, 2^b, 2^a + 2^b), with two distinct bits a, b drawn per run; the stored order is a random permutation of the pattern. Every tile-column holds exactly 4 stored tiles; no (tile_row, tile_column) pair appears twice.
All inputs are finite; a program needn't handle non-finite values.
Results may differ from the reference program's by a relative error of at most 0.0034.
Values may be sent and summed in bfloat16 or wider, within the bound.
No kernel may reach another device: no remote copies, remote signals or barrier semaphores. Data moves between devices by JAX's collectives and lax.ppermute only.
A program may use at most 128 MiB of HBM per device.

```python
import math
import jax
import jax.numpy as jnp
from jax import lax

WIDTH = 8192
TILE = 128
PER_ROW = 4
ROWS_DEV = 192
BLOCKS = 64
NTILES = 256
ROWS = 49152
N_DP = 16
N_FSDP = 16


def butterfly(key):
    blocks = WIDTH // TILE
    levels = blocks.bit_length() - 1
    chosen = jax.random.permutation(jax.random.fold_in(key, 7), levels)[:2].astype(jnp.int32)
    first_bit = jnp.left_shift(jnp.int32(1), chosen[0])
    second_bit = jnp.left_shift(jnp.int32(1), chosen[1])
    masks = jnp.stack([jnp.int32(0) * first_bit, first_bit, second_bit, first_bit + second_bit]).astype(jnp.int32)
    row_list = jnp.repeat(jnp.arange(blocks, dtype=jnp.int32), PER_ROW)
    column_list = jnp.bitwise_xor(row_list, jnp.tile(masks, blocks))
    shuffle = jax.random.permutation(jax.random.fold_in(key, 11), NTILES)
    return (row_list[shuffle].astype(jnp.int32), column_list[shuffle].astype(jnp.int32))


def draw_tile_row(key, part):
    return butterfly(key)[0]


def draw_tile_column(key, part):
    return butterfly(key)[1]


def shard_levels(key, dims, split, low, high):
    def one(position, blocks):
        draws = jax.random.uniform(jax.random.fold_in(jax.random.fold_in(key, 6), position), (blocks,), jnp.float32, low / len(split), high / len(split))
        return jnp.repeat(jnp.exp(draws), dims[position] // blocks).reshape((-1,) + (1,) * (len(dims) - position - 1))

    factor_of = one(*split[0])
    for cut in split[1:]:
        factor_of = factor_of * one(*cut)
    return factor_of


def scatter_about(stream_key, extent, deviation, bound, shards=(), held_as=jnp.bfloat16):
    level = shard_levels(stream_key, extent, shards, -0.22, 0.18) if shards else 1.0
    values = jax.random.normal(stream_key, extent, jnp.float32) * deviation * level
    return jnp.minimum(jnp.maximum(values, -bound), bound).astype(held_as)


def setup_inputs(seed: int = 0) -> dict:
    key_of = jax.random.split(jax.random.key(seed), 6)
    features = scatter_about(key_of[0], (ROWS, WIDTH), 1.0, 6.0, ((0, 256),))
    grad_out = scatter_about(key_of[1], (ROWS, WIDTH), 1.0, 6.0, ((0, 256),))
    weight_tiles = scatter_about(key_of[2], (NTILES, TILE, TILE), (PER_ROW * TILE) ** -0.5, 0.25, ((0, 16),))
    tile_row = draw_tile_row(jax.random.fold_in(key_of[5], 71), 0)
    tile_column = draw_tile_column(jax.random.fold_in(key_of[5], 71), 0)
    return {"features": features, "grad_out": grad_out, "weight_tiles": weight_tiles, "tile_row": tile_row, "tile_column": tile_column}


def gelu_slope(value):
    root_term = math.sqrt(2.0 / math.pi)
    inner = root_term * (value + 0.044715 * value * value * value)
    hyper = jnp.tanh(inner)
    return 0.5 * (1.0 + hyper) + 0.5 * value * (1.0 - hyper * hyper) * root_term * (1.0 + 3.0 * 0.044715 * value * value)

def reference(features, grad_out, weight_tiles, tile_row, tile_column):
    devices_all = N_DP * N_FSDP
    ordering = jnp.argsort(tile_row, stable=True)
    sorted_columns = tile_column[ordering].reshape(BLOCKS, PER_ROW)
    sorted_tiles = weight_tiles[ordering].astype(jnp.float32).reshape(BLOCKS, PER_ROW, TILE, TILE)
    feature_dev = features.reshape(devices_all, ROWS_DEV, BLOCKS, TILE)
    grad_dev = grad_out.reshape(devices_all, ROWS_DEV, BLOCKS, TILE)

    def per_device(total, inputs):
        feature_blocks, grad_blocks = inputs
        gathered = feature_blocks[:, sorted_columns].astype(jnp.float32)
        preact = jnp.einsum('rnkc,nkcd->rnd', gathered, sorted_tiles)
        slope_grad = (grad_blocks.astype(jnp.float32) * gelu_slope(preact)).astype(jnp.bfloat16)
        returned = jnp.einsum('rnd,nkcd->rnkc', slope_grad.astype(jnp.float32), sorted_tiles)
        spread = jnp.zeros((ROWS_DEV, BLOCKS, TILE), jnp.float32).at[:, sorted_columns].add(returned)
        grad_rows = (grad_blocks.astype(jnp.float32) + spread).astype(jnp.bfloat16)
        partial_value = jnp.einsum('rtc,rtd->tcd', feature_blocks[:, tile_column].astype(jnp.float32), slope_grad[:, tile_row].astype(jnp.float32))
        return (total + partial_value, grad_rows)
    weight_grad, grad_rows = lax.scan(per_device, jnp.zeros((NTILES, TILE, TILE), jnp.float32), (feature_dev, grad_dev))
    grad_features = grad_rows.reshape(ROWS, WIDTH)
    tile_update = weight_grad * lax.rsqrt(lax.optimization_barrier(jnp.mean(weight_grad * weight_grad, axis=(1, 2), keepdims=True)) + 1e-06)
    return (grad_features, tile_update)
```

```python
import functools
import math

import jax
import jax.numpy as jnp
from jax import lax
from jax.experimental import pallas as pl
from jax.experimental.pallas import tpu as pltpu
from jax.sharding import Mesh
from jax.sharding import PartitionSpec as P

AXES = ("zh", "y", "x", "zl", "core")
SIZES = (4, 4, 4, 2, 2)
SIDE = 128
ROOT = math.sqrt(2.0 / math.pi)
CUBIC = 0.044715

VMEM = pl.BlockSpec(memory_space=pltpu.VMEM)
SMEM = pl.BlockSpec(memory_space=pltpu.SMEM)
PARAMS = pltpu.CompilerParams(vmem_limit_bytes=52 * 1024 * 1024)


def shape(dims, dtype):
    return jax.ShapeDtypeStruct(dims, dtype)


def lanes(block):
    return pl.ds(pl.multiple_of(block * SIDE, SIDE), SIDE)


def slope_times(value, cotangent):
    square = value * value
    hyper = jnp.tanh(value * (ROOT + (ROOT * CUBIC) * square))
    slope = 0.5 * (1.0 + hyper) + (0.5 * value) * (1.0 - hyper * hyper) * (
        ROOT + (3.0 * ROOT * CUBIC) * square
    )
    return cotangent * slope


def forward_kernel(place, blocks, x_ref, g_ref, w_ref, s_ref):
    def one(group, carry):
        ids = [blocks[group * 4 + m] for m in range(4)]
        x = jnp.concatenate([x_ref[:, lanes(b)] for b in ids], axis=1)
        for first in (0, 2):
            pair = (first, first + 1)
            w = jnp.concatenate(
                [
                    jnp.concatenate([w_ref[place[ids[n] * 4 + (n ^ m)]] for n in pair], axis=1)
                    for m in range(4)
                ],
                axis=0,
            )
            pre = jnp.dot(x, w, preferred_element_type=jnp.float32)
            for k, n in enumerate(pair):
                cot = g_ref[:, lanes(ids[n])].astype(jnp.float32)
                out = slope_times(pre[:, k * SIDE : (k + 1) * SIDE], cot)
                s_ref[ids[n]] = out.astype(jnp.bfloat16)
        return carry

    lax.fori_loop(0, 16, one, 0)


def backward_kernel(place, blocks, g_ref, w_ref, s_ref, o_ref):
    def one(group, carry):
        ids = [blocks[group * 4 + m] for m in range(4)]
        s = jnp.concatenate([s_ref[b] for b in ids], axis=1)
        for first in (0, 2):
            pair = (first, first + 1)
            w = jnp.concatenate(
                [
                    jnp.concatenate(
                        [w_ref[place[ids[n] * 4 + (n ^ m)]] for n in range(4)], axis=1
                    )
                    for m in pair
                ],
                axis=0,
            )
            back = lax.dot_general(
                s, w, (((1,), (1,)), ((), ())), preferred_element_type=jnp.float32
            )
            for k, m in enumerate(pair):
                cot = g_ref[:, lanes(ids[m])].astype(jnp.float32)
                total = cot + back[:, k * SIDE : (k + 1) * SIDE]
                o_ref[:, lanes(ids[m])] = total.astype(jnp.bfloat16)
        return carry

    lax.fori_loop(0, 16, one, 0)


def transpose_kernel(mine_ref, other_ref, xt_ref):
    def one(block, carry):
        rows = jnp.concatenate([mine_ref[:, lanes(block)], other_ref[:, lanes(block)]], axis=0)
        xt_ref[block] = rows.T
        return carry

    lax.fori_loop(0, 64, one, 0)


GROUPS = (("x", 0), ("x", 1), ("y", 0), ("y", 1))
SENT = ((1, 2), (3, 2))
KEPT = ((0, 3), (0, 1))


def partial_kernel(which, splits, rows, cols, where, xt_ref, s_ref, t_ref, *outs):
    x, y, zl, core = where[0], where[1], where[2], where[3]
    for group, (axis, half) in enumerate(GROUPS):
        for p, rel in enumerate(which[half]):
            for other in range(4):
                for low in range(2):
                    rx, ry = (rel, other) if axis == "x" else (other, rel)
                    to_zl = (1 - zl) if axis == "x" else zl
                    k = (y ^ ry) * 4 + half * 2 + low
                    tile = (((x ^ rx) * 2 + to_zl) * 2 + core) * 16 + k
                    row, col = rows[tile], cols[tile]
                    s = jnp.concatenate([s_ref[row], t_ref[row]], axis=0)
                    value = jnp.dot(xt_ref[col], s, preferred_element_type=jnp.float32)
                    if splits:
                        out, at = outs[group * 2 + p], other * 2 + low
                    else:
                        out, at = outs[group], p * 8 + other * 2 + low
                    out[at] = value.astype(out.dtype)


def finish_kernel(where, *refs):
    out = refs[-1]
    y = where[1]
    for r in range(4):
        for k in range(4):
            grad = refs[r][k]
            mean = jnp.mean(grad * grad)
            out[(y ^ r) * 4 + k] = grad * lax.rsqrt(mean + 1e-06)


def sum_four_kernel(a, b, c, d, out):
    f32 = jnp.float32
    out[...] = (a[...].astype(f32) + b[...].astype(f32)) + (
        c[...].astype(f32) + d[...].astype(f32)
    )


def swap(value, axis, mask):
    size = SIZES[AXES.index(axis)]
    return lax.ppermute(value, axis, [(i, i ^ mask) for i in range(size)])


def tables(tile_row, tile_column):
    differ = tile_row ^ tile_column
    both = lax.reduce(differ, jnp.int32(0), lax.bitwise_or, (0,))
    low = both & -both
    high = both ^ low
    kind = jnp.where((differ & low) != 0, 1, 0) + jnp.where((differ & high) != 0, 2, 0)
    slot = tile_row * 4 + kind
    index = jnp.arange(256, dtype=jnp.int32)
    place = jnp.sum(jnp.where(slot[None, :] == index[:, None], index[None, :], 0), axis=1)
    group = jnp.arange(16, dtype=jnp.int32)
    base = group + (group & ~(low - 1))
    base = base + (base & ~(high - 1))
    member = jnp.stack([0 * low, low, high, both])
    blocks = (base[:, None] ^ member[None, :]).reshape(64)
    return place.astype(jnp.int32), blocks.astype(jnp.int32)


def on_device(features, grad_out, weight_tiles, tile_row, tile_column):
    bf16, f32 = jnp.bfloat16, jnp.float32
    tile_row = tile_row.astype(jnp.int32)
    tile_column = tile_column.astype(jnp.int32)
    rows_here = features.shape[0]
    where = jnp.stack([lax.axis_index(a) for a in ("x", "y", "zl", "core")]).astype(jnp.int32)
    whole = lax.all_gather(weight_tiles, ("x", "zl", "core"), axis=0, tiled=True)
    others = swap(features, "core", 1)
    xt = pl.pallas_call(
        transpose_kernel,
        out_shape=shape((64, SIDE, 2 * rows_here), bf16),
        in_specs=[VMEM, VMEM],
        out_specs=VMEM,
        compiler_params=PARAMS,
    )(features, others)
    place, blocks = tables(tile_row, tile_column)
    slopes = pl.pallas_call(
        forward_kernel,
        out_shape=shape((64, rows_here, SIDE), bf16),
        in_specs=[SMEM, SMEM, VMEM, VMEM, VMEM],
        out_specs=VMEM,
        compiler_params=PARAMS,
    )(place, blocks, features, grad_out, whole)
    other_slopes = swap(slopes, "core", 1)
    operands = (tile_row, tile_column, where, xt, slopes, other_slopes)
    sent = pl.pallas_call(
        functools.partial(partial_kernel, SENT, False),
        out_shape=[shape((16, SIDE, SIDE), bf16)] * 4,
        in_specs=[SMEM] * 3 + [VMEM] * 3,
        out_specs=[VMEM] * 4,
        compiler_params=PARAMS,
    )(*operands)
    got = [
        swap(value, axis, (1, 3)[half]) for value, (axis, half) in zip(sent, GROUPS, strict=True)
    ]
    kept = pl.pallas_call(
        functools.partial(partial_kernel, KEPT, True),
        out_shape=[shape((8, SIDE, SIDE), f32)] * 8,
        in_specs=[SMEM] * 3 + [VMEM] * 3,
        out_specs=[VMEM] * 8,
        compiler_params=PARAMS,
    )(*operands)
    grad_features = pl.pallas_call(
        backward_kernel,
        out_shape=shape(features.shape, bf16),
        in_specs=[SMEM, SMEM, VMEM, VMEM, VMEM],
        out_specs=VMEM,
        compiler_params=PARAMS,
    )(place, blocks, grad_out, whole, slopes)

    second = [
        swap((kept[2 * i + 1] + got[i][8:].astype(f32)).astype(bf16), axis, (3, 1)[half])
        for i, (axis, half) in enumerate(GROUPS)
    ]
    held = [
        kept[2 * i] + got[i][:8].astype(f32) + second[i].astype(f32) for i in range(4)
    ]
    pieces = []
    for i, axis in ((0, "y"), (2, "x")):
        both = jnp.concatenate(
            [held[i].reshape(4, 2, SIDE, SIDE), held[i + 1].reshape(4, 2, SIDE, SIDE)], axis=1
        )
        away = [swap(both[r].astype(bf16), axis, r) for r in (1, 3, 2)]
        pieces.append(
            both[0] + (away[0].astype(f32) + away[1].astype(f32)) + away[2].astype(f32)
        )
    mine = (pieces[1] + swap(pieces[0], "zl", 1)).astype(bf16)
    across = [swap(mine, "zh", r) for r in (1, 2, 3)]
    summed = pl.pallas_call(
        sum_four_kernel,
        out_shape=shape((4, SIDE, SIDE), f32),
        in_specs=[VMEM] * 4,
        out_specs=VMEM,
        compiler_params=PARAMS,
    )(mine, *across)
    gathered = [swap(summed, "y", r) for r in (1, 2, 3)]
    tile_update = pl.pallas_call(
        finish_kernel,
        out_shape=shape((16, SIDE, SIDE), f32),
        in_specs=[SMEM] + [VMEM] * 4,
        out_specs=VMEM,
        compiler_params=PARAMS,
    )(where, summed, *gathered)
    return grad_features, tile_update


def solution(mesh):
    grid = Mesh(mesh.devices.reshape(SIZES), AXES)
    return jax.shard_map(
        on_device,
        mesh=grid,
        in_specs=(P(AXES, None), P(AXES, None), P(("x", "zl", "core"), None, None), P(), P()),
        out_specs=(P(AXES, None), P(("x", "zl", "core"), None, None)),
        check_vma=False,
    )
```

```python
import functools
import math

import jax
import jax.numpy as jnp
from jax import lax
from jax.experimental import pallas as pl
from jax.experimental.pallas import tpu as pltpu
from jax.sharding import Mesh
from jax.sharding import PartitionSpec as P

AXES = ("zh", "y", "x", "zl", "core")
SIZES = (4, 4, 4, 2, 2)
SIDE = 128
ROOT = math.sqrt(2.0 / math.pi)
CUBIC = 0.044715
UNROLL = 2

VMEM = pl.BlockSpec(memory_space=pltpu.VMEM)
SMEM = pl.BlockSpec(memory_space=pltpu.SMEM)
ANY = pl.BlockSpec(memory_space=pl.ANY)
Z = ("zh", "zl")
PARAMS = pltpu.CompilerParams(vmem_limit_bytes=8 * 1024 * 1024)


def shape(dims, dtype):
    return jax.ShapeDtypeStruct(dims, dtype)


def near(value):
    return pltpu.with_memory_space_constraint(value, pltpu.VMEM)


def stored(value):
    return pltpu.with_memory_space_constraint(value, pltpu.HBM)


def lanes(block):
    return pl.ds(pl.multiple_of(block * SIDE, SIDE), SIDE)


def slope_times(value, cotangent):
    square = value * value
    hyper = jnp.tanh(value * (ROOT + (ROOT * CUBIC) * square))
    slope = 0.5 * (1.0 + hyper) + (0.5 * value) * (1.0 - hyper * hyper) * (
        ROOT + (3.0 * ROOT * CUBIC) * square
    )
    return cotangent * slope


PIECES = tuple(
    (x, zl, core, first, size)
    for core in (0, 1)
    for x, zl, first, size in (
        (0, 0, 0, 16),
        (3, 0, 0, 16),
        (1, 0, 0, 16),
        (0, 1, 0, 16),
        (3, 1, 0, 16),
        (1, 1, 0, 16),
        (2, 0, 0, 16),
        (2, 1, 0, 8),
        (2, 1, 8, 8),
    )
)


def forward_kernel(where, place, blocks, x_ref, g_ref, *refs):
    pieces, (s_ref, w_ref, sems) = refs[: len(PIECES)], refs[len(PIECES) :]
    copies = []
    for i, (x, zl, core, first, size) in enumerate(PIECES):
        owner = (lax.rem(where[0] + x, 4) * 2 + (where[2] ^ zl)) * 2 + (where[3] ^ core)
        copies.append(
            pltpu.make_async_copy(
                pieces[i], w_ref.at[pl.ds(owner * 16 + first, size)], sems.at[i]
            )
        )
    for copy in copies:
        copy.start()
    for copy in copies:
        copy.wait()

    def one(group):
        ids = [blocks[group * 4 + m] for m in range(4)]
        x = jnp.concatenate([x_ref[:, lanes(b)] for b in ids], axis=1)
        for first in (0, 2):
            pair = (first, first + 1)
            w = jnp.concatenate(
                [
                    jnp.concatenate([w_ref[place[ids[n] * 4 + (n ^ m)]] for n in pair], axis=1)
                    for m in range(4)
                ],
                axis=0,
            )
            pre = jnp.dot(x, w, preferred_element_type=jnp.float32)
            for k, n in enumerate(pair):
                cot = g_ref[:, lanes(ids[n])].astype(jnp.float32)
                out = slope_times(pre[:, k * SIDE : (k + 1) * SIDE], cot)
                s_ref[ids[n]] = out.astype(jnp.bfloat16)

    def some(step, carry):
        for k in range(UNROLL):
            one(step * UNROLL + k)
        return carry

    lax.fori_loop(0, 16 // UNROLL, some, 0)


def backward_kernel(place, blocks, g_ref, w_ref, s_ref, o_ref):
    def one(group, carry):
        ids = [blocks[group * 4 + m] for m in range(4)]
        s = jnp.concatenate([s_ref[b] for b in ids], axis=1)
        for first in (0, 2):
            pair = (first, first + 1)
            w = jnp.concatenate(
                [
                    jnp.concatenate(
                        [w_ref[place[ids[n] * 4 + (n ^ m)]] for n in range(4)], axis=1
                    )
                    for m in pair
                ],
                axis=0,
            )
            back = lax.dot_general(
                s, w, (((1,), (1,)), ((), ())), preferred_element_type=jnp.float32
            )
            for k, m in enumerate(pair):
                cot = g_ref[:, lanes(ids[m])].astype(jnp.float32)
                total = cot + back[:, k * SIDE : (k + 1) * SIDE]
                o_ref[:, lanes(ids[m])] = total.astype(jnp.bfloat16)
        return carry

    lax.fori_loop(0, 16, one, 0)


def transpose_kernel(mine_ref, other_ref, xt_ref):
    def one(block, carry):
        rows = jnp.concatenate([mine_ref[:, lanes(block)], other_ref[:, lanes(block)]], axis=0)
        xt_ref[block] = rows.T
        return carry

    lax.fori_loop(0, 64, one, 0)


GROUPS = (("x", 0), ("x", 1), ("y", 0), ("y", 1))
SENT = ((1, 2), (3, 2))
KEPT = ((0, 3), (0, 1))


def partial_kernel(which, splits, rows, cols, where, xt_ref, s_ref, t_ref, *outs):
    x, y, zl, core = where[0], where[1], where[2], where[3]
    for group, (axis, half) in enumerate(GROUPS):
        for p, rel in enumerate(which[half]):
            for other in range(4):
                for low in range(2):
                    rx, ry = (rel, other) if axis == "x" else (other, rel)
                    to_zl = (1 - zl) if axis == "x" else zl
                    k = (y ^ ry) * 4 + half * 2 + low
                    tile = (((x ^ rx) * 2 + to_zl) * 2 + core) * 16 + k
                    row, col = rows[tile], cols[tile]
                    s = jnp.concatenate([s_ref[row], t_ref[row]], axis=0)
                    value = jnp.dot(xt_ref[col], s, preferred_element_type=jnp.float32)
                    if splits:
                        out, at = outs[group * 2 + p], other * 2 + low
                    else:
                        out, at = outs[group], p * 8 + other * 2 + low
                    out[at] = value.astype(out.dtype)


def finish_kernel(where, *refs):
    out = refs[-1]
    y = where[1]
    for r in range(4):
        for k in range(4):
            grad = refs[r][k]
            mean = jnp.mean(grad * grad)
            out[(y ^ r) * 4 + k] = grad * lax.rsqrt(mean + 1e-06)


def sum_four_kernel(a, b, c, d, out):
    f32 = jnp.float32
    out[...] = (a[...].astype(f32) + b[...].astype(f32)) + (
        c[...].astype(f32) + d[...].astype(f32)
    )


def swap(value, axis, mask):
    size = SIZES[AXES.index(axis)]
    return lax.ppermute(value, axis, [(i, i ^ mask) for i in range(size)])


def turn(value, axes, by):
    names = axes if isinstance(axes, tuple) else (axes,)
    size = math.prod(SIZES[AXES.index(name)] for name in names)
    return lax.ppermute(value, axes, [(i, (i + by) % size) for i in range(size)])


def tables(tile_row, tile_column):
    differ = tile_row ^ tile_column
    both = lax.reduce(differ, jnp.int32(0), lax.bitwise_or, (0,))
    low = both & -both
    high = both ^ low
    kind = jnp.where((differ & low) != 0, 1, 0) + jnp.where((differ & high) != 0, 2, 0)
    slot = tile_row * 4 + kind
    index = jnp.arange(256, dtype=jnp.int32)
    place = jnp.sum(jnp.where(slot[None, :] == index[:, None], index[None, :], 0), axis=1)
    group = jnp.arange(16, dtype=jnp.int32)
    base = group + (group & ~(low - 1))
    base = base + (base & ~(high - 1))
    member = jnp.stack([0 * low, low, high, both])
    blocks = (base[:, None] ^ member[None, :]).reshape(64)
    return place.astype(jnp.int32), blocks.astype(jnp.int32)


def on_device(features, grad_out, weight_tiles, tile_row, tile_column):
    bf16, f32 = jnp.bfloat16, jnp.float32
    tile_row = tile_row.astype(jnp.int32)
    tile_column = tile_column.astype(jnp.int32)
    rows_here = features.shape[0]
    where = jnp.stack([lax.axis_index(a) for a in ("x", "y", "zl", "core")]).astype(jnp.int32)
    place, blocks = tables(tile_row, tile_column)
    own = weight_tiles
    left, right = turn(own, "x", 1), turn(own, "x", 3)
    beside = swap(own, "zl", 1)
    others = swap(features, "core", 1)
    far = turn(left, "x", 1)
    beside_left, beside_right = turn(left, Z, 1), turn(right, Z, 7)
    features_near, grad_out = near(features), near(grad_out)
    beside_far = (turn(far[:8], Z, 1), turn(far[8:], Z, 7))
    mine = (own, left, right, beside, beside_left, beside_right, far, *beside_far)
    pieces = (*mine, *(swap(piece, "core", 1) for piece in mine))
    pieces = [stored(piece) for piece in pieces]
    slopes, whole = pl.pallas_call(
        forward_kernel,
        out_shape=[
            pltpu.VMEM((64, rows_here, SIDE), bf16),
            pltpu.VMEM((256, SIDE, SIDE), bf16),
        ],
        in_specs=[SMEM] * 3 + [VMEM] * 2 + [ANY] * len(pieces),
        out_specs=[VMEM, VMEM],
        scratch_shapes=[pltpu.SemaphoreType.DMA((len(pieces),))],
        compiler_params=PARAMS,
    )(where, place, blocks, features_near, grad_out, *pieces)
    slopes, others = lax.optimization_barrier((slopes, others))
    other_slopes = swap(slopes, "core", 1)
    xt = pl.pallas_call(
        transpose_kernel,
        out_shape=pltpu.VMEM((64, SIDE, 2 * rows_here), bf16),
        in_specs=[VMEM, VMEM],
        out_specs=VMEM,
        compiler_params=PARAMS,
    )(features_near, near(others))
    operands = (tile_row, tile_column, where, near(xt), near(slopes), near(other_slopes))
    sent = pl.pallas_call(
        functools.partial(partial_kernel, SENT, False),
        out_shape=[shape((16, SIDE, SIDE), bf16)] * 4,
        in_specs=[SMEM] * 3 + [VMEM] * 3,
        out_specs=[VMEM] * 4,
        compiler_params=PARAMS,
    )(*operands)
    got = [
        swap(value, axis, (1, 3)[half]) for value, (axis, half) in zip(sent, GROUPS, strict=True)
    ]
    kept = pl.pallas_call(
        functools.partial(partial_kernel, KEPT, True),
        out_shape=[shape((8, SIDE, SIDE), f32)] * 8,
        in_specs=[SMEM] * 3 + [VMEM] * 3,
        out_specs=[VMEM] * 8,
        compiler_params=PARAMS,
    )(*operands)
    grad_features = pl.pallas_call(
        backward_kernel,
        out_shape=shape(features.shape, bf16),
        in_specs=[SMEM, SMEM, VMEM, VMEM, VMEM],
        out_specs=VMEM,
        compiler_params=PARAMS,
    )(place, blocks, grad_out, near(whole), near(slopes))

    second = [
        swap((kept[2 * i + 1] + got[i][8:].astype(f32)).astype(bf16), axis, (3, 1)[half])
        for i, (axis, half) in enumerate(GROUPS)
    ]
    held = [
        kept[2 * i] + got[i][:8].astype(f32) + second[i].astype(f32) for i in range(4)
    ]
    rest = [
        jnp.concatenate(
            [held[i].reshape(4, 2, SIDE, SIDE), held[i + 1].reshape(4, 2, SIDE, SIDE)], axis=1
        )
        for i in (0, 2)
    ]
    away = [swap(rest[0][r].astype(bf16), "y", r) for r in (1, 2, 3)]
    away += [swap(rest[1][r].astype(bf16), "x", r) for r in (1, 2, 3)]
    away = [piece.astype(f32) for piece in lax.optimization_barrier(away)]
    sums = [rest[i][0] + (away[3 * i] + away[3 * i + 2]) + away[3 * i + 1] for i in (0, 1)]
    mine = (sums[1] + swap(sums[0], "zl", 1)).astype(bf16)
    across = [swap(mine, "zh", r) for r in (1, 2, 3)]
    summed = pl.pallas_call(
        sum_four_kernel,
        out_shape=shape((4, SIDE, SIDE), f32),
        in_specs=[VMEM] * 4,
        out_specs=VMEM,
        compiler_params=PARAMS,
    )(mine, *across)
    gathered = [swap(summed, "y", r) for r in (1, 2, 3)]
    tile_update = pl.pallas_call(
        finish_kernel,
        out_shape=shape((16, SIDE, SIDE), f32),
        in_specs=[SMEM] + [VMEM] * 4,
        out_specs=VMEM,
        compiler_params=PARAMS,
    )(where, summed, *gathered)
    return grad_features, tile_update


def solution(mesh):
    grid = Mesh(mesh.devices.reshape(SIZES), AXES)
    return jax.shard_map(
        on_device,
        mesh=grid,
        in_specs=(P(AXES, None), P(AXES, None), P(("x", "zl", "core"), None, None), P(), P()),
        out_specs=(P(AXES, None), P(("x", "zl", "core"), None, None)),
        check_vma=False,
    )
```

```python
import functools
import math

import jax
import jax.numpy as jnp
from jax import lax
from jax.experimental import pallas as pl
from jax.experimental.pallas import tpu as pltpu
from jax.sharding import Mesh
from jax.sharding import PartitionSpec as P

AXES = ("zh", "y", "x", "zl", "core")
SIZES = (4, 4, 4, 2, 2)
SIDE = 128
ROOT = math.sqrt(2.0 / math.pi)
CUBIC = 0.044715
UNROLL = 2

VMEM = pl.BlockSpec(memory_space=pltpu.VMEM)
SMEM = pl.BlockSpec(memory_space=pltpu.SMEM)
ANY = pl.BlockSpec(memory_space=pl.ANY)
Z = ("zh", "zl")
PARAMS = pltpu.CompilerParams(vmem_limit_bytes=8 * 1024 * 1024)


def shape(dims, dtype):
    return jax.ShapeDtypeStruct(dims, dtype)


def near(value):
    return pltpu.with_memory_space_constraint(value, pltpu.VMEM)


def stored(value):
    return pltpu.with_memory_space_constraint(value, pltpu.HBM)


def lanes(block):
    return pl.ds(pl.multiple_of(block * SIDE, SIDE), SIDE)


def slope_times(value, cotangent):
    square = value * value
    hyper = jnp.tanh(value * (ROOT + (ROOT * CUBIC) * square))
    slope = 0.5 * (1.0 + hyper) + (0.5 * value) * (1.0 - hyper * hyper) * (
        ROOT + (3.0 * ROOT * CUBIC) * square
    )
    return cotangent * slope


ROUNDS = (
    (0, 0, 0, 16),
    (3, 0, 0, 16),
    (1, 0, 0, 16),
    (0, 1, 0, 16),
    (3, 1, 0, 16),
    (1, 1, 0, 16),
    (2, 0, 0, 8),
    (2, 0, 8, 8),
    (2, 1, 0, 8),
    (2, 1, 8, 8),
)
FIRST = tuple((*ROUNDS[i][:2], 0, *ROUNDS[i][2:]) for i in range(4)) + ((0, 0, 1, 0, 16),)
MIDDLE = (
    *((*ROUNDS[i][:2], 0, *ROUNDS[i][2:]) for i in range(4, 8)),
    *((*ROUNDS[i][:2], 1, *ROUNDS[i][2:]) for i in range(1, 4)),
    (2, 0, 1, 0, 16),
)
LAST = (
    *((*ROUNDS[i][:2], 0, *ROUNDS[i][2:]) for i in (8, 9)),
    *((*ROUNDS[i][:2], 1, *ROUNDS[i][2:]) for i in (4, 5, 8, 9)),
)


def place_copies(where, listed, pieces, w_ref, sems):
    copies = []
    for i, (x, zl, core, first, size) in enumerate(listed):
        owner = (lax.rem(where[0] + x, 4) * 2 + (where[2] ^ zl)) * 2 + (where[3] ^ core)
        to = w_ref.at[pl.ds(owner * 16 + first, size)]
        copies.append(pltpu.make_async_copy(pieces[i], to, sems.at[i]))
    return copies


def run(copies):
    for copy in copies:
        copy.start()
    for copy in copies:
        copy.wait()


def load_kernel(where, x_hbm, g_hbm, *refs):
    pieces, (x_ref, g_ref, w_ref, sems) = refs[: len(FIRST)], refs[len(FIRST) :]
    copies = place_copies(where, FIRST, pieces, w_ref, sems)
    copies.append(pltpu.make_async_copy(x_hbm, x_ref, sems.at[len(FIRST)]))
    copies.append(pltpu.make_async_copy(g_hbm, g_ref, sems.at[len(FIRST) + 1]))
    run(copies)


def more_kernel(where, given, *refs):
    del given
    pieces, (w_ref, sems) = refs[: len(MIDDLE)], refs[len(MIDDLE) :]
    run(place_copies(where, MIDDLE, pieces, w_ref, sems))


def forward_kernel(where, place, blocks, x_ref, g_ref, given, *refs):
    del given
    pieces, (s_ref, w_ref, sems) = refs[: len(LAST)], refs[len(LAST) :]
    run(place_copies(where, LAST, pieces, w_ref, sems))

    def one(group):
        ids = [blocks[group * 4 + m] for m in range(4)]
        x = jnp.concatenate([x_ref[:, lanes(b)] for b in ids], axis=1)
        for first in (0, 2):
            pair = (first, first + 1)
            w = jnp.concatenate(
                [
                    jnp.concatenate([w_ref[place[ids[n] * 4 + (n ^ m)]] for n in pair], axis=1)
                    for m in range(4)
                ],
                axis=0,
            )
            pre = jnp.dot(x, w, preferred_element_type=jnp.float32)
            for k, n in enumerate(pair):
                cot = g_ref[:, lanes(ids[n])].astype(jnp.float32)
                out = slope_times(pre[:, k * SIDE : (k + 1) * SIDE], cot)
                s_ref[ids[n]] = out.astype(jnp.bfloat16)

    def some(step, carry):
        for k in range(UNROLL):
            one(step * UNROLL + k)
        return carry

    lax.fori_loop(0, 16 // UNROLL, some, 0)


def backward_kernel(half, place, blocks, g_ref, w_ref, s_ref, *refs):
    o_hbm, out, sems = refs[-3:]

    def write(at, column):
        return pltpu.make_async_copy(out.at[at], o_hbm.at[:, lanes(column)], sems.at[at])

    def one(step, carry):
        ids = [blocks[(half * 8 + step) * 4 + m] for m in range(4)]
        s = jnp.concatenate([s_ref[b] for b in ids], axis=1)
        for first in (0, 2):
            pair = (first, first + 1)
            w = jnp.concatenate(
                [
                    jnp.concatenate(
                        [w_ref[place[ids[n] * 4 + (n ^ m)]] for n in range(4)], axis=1
                    )
                    for m in pair
                ],
                axis=0,
            )
            back = lax.dot_general(
                s, w, (((1,), (1,)), ((), ())), preferred_element_type=jnp.float32
            )
            for k, m in enumerate(pair):
                cot = g_ref[:, lanes(ids[m])].astype(jnp.float32)
                total = cot + back[:, k * SIDE : (k + 1) * SIDE]
                out[step * 4 + m] = total.astype(jnp.bfloat16)
        for m in range(4):
            write(step * 4 + m, ids[m]).start()
        return carry

    def done(at, carry):
        write(at, blocks[half * 32 + at]).wait()
        return carry

    lax.fori_loop(0, 8, one, 0)
    lax.fori_loop(0, 32, done, 0)


def transpose_kernel(mine_ref, other_ref, xt_ref):
    def one(block, carry):
        rows = jnp.concatenate([mine_ref[:, lanes(block)], other_ref[:, lanes(block)]], axis=0)
        xt_ref[block] = rows.T
        return carry

    lax.fori_loop(0, 64, one, 0)


GROUPS = (("x", 0), ("x", 1), ("y", 0), ("y", 1))
SENT = ((1, 2), (3, 2))
KEPT = ((0, 3), (0, 1))


def partial_kernel(which, splits, rows, cols, where, xt_ref, s_ref, t_ref, *outs):
    x, y, zl, core = where[0], where[1], where[2], where[3]
    for group, (axis, half) in enumerate(GROUPS):
        for p, rel in enumerate(which[half]):
            for other in range(4):
                for low in range(2):
                    rx, ry = (rel, other) if axis == "x" else (other, rel)
                    to_zl = (1 - zl) if axis == "x" else zl
                    k = (y ^ ry) * 4 + half * 2 + low
                    tile = (((x ^ rx) * 2 + to_zl) * 2 + core) * 16 + k
                    row, col = rows[tile], cols[tile]
                    s = jnp.concatenate([s_ref[row], t_ref[row]], axis=0)
                    value = jnp.dot(xt_ref[col], s, preferred_element_type=jnp.float32)
                    if splits:
                        out, at = outs[group * 2 + p], other * 2 + low
                    else:
                        out, at = outs[group], p * 8 + other * 2 + low
                    out[at] = value.astype(out.dtype)


def normalize_kernel(a, b, c, d, out):
    f32 = jnp.float32
    for k in range(4):
        grad = (a[k].astype(f32) + b[k].astype(f32)) + (c[k].astype(f32) + d[k].astype(f32))
        mean = jnp.mean(grad * grad)
        out[k] = (grad * lax.rsqrt(mean + 1e-06)).astype(jnp.bfloat16)


def finish_kernel(where, *refs):
    for r in range(4):
        for k in range(4):
            refs[-1][(where[1] ^ r) * 4 + k] = refs[r][k].astype(jnp.float32)


def swap(value, axis, mask):
    size = SIZES[AXES.index(axis)]
    return lax.ppermute(value, axis, [(i, i ^ mask) for i in range(size)])


def turn(value, axes, by):
    names = axes if isinstance(axes, tuple) else (axes,)
    size = math.prod(SIZES[AXES.index(name)] for name in names)
    return lax.ppermute(value, axes, [(i, (i + by) % size) for i in range(size)])


def tables(tile_row, tile_column):
    differ = tile_row ^ tile_column
    both = lax.reduce(differ, jnp.int32(0), lax.bitwise_or, (0,))
    low = both & -both
    high = both ^ low
    kind = jnp.where((differ & low) != 0, 1, 0) + jnp.where((differ & high) != 0, 2, 0)
    slot = tile_row * 4 + kind
    index = jnp.arange(256, dtype=jnp.int32)
    place = jnp.sum(jnp.where(slot[None, :] == index[:, None], index[None, :], 0), axis=1)
    group = jnp.arange(16, dtype=jnp.int32)
    base = group + (group & ~(low - 1))
    base = base + (base & ~(high - 1))
    member = jnp.stack([0 * low, low, high, both])
    blocks = (base[:, None] ^ member[None, :]).reshape(64)
    return place.astype(jnp.int32), blocks.astype(jnp.int32)


def on_device(features, grad_out, weight_tiles, tile_row, tile_column):
    bf16, f32 = jnp.bfloat16, jnp.float32
    tile_row = tile_row.astype(jnp.int32)
    tile_column = tile_column.astype(jnp.int32)
    rows_here = features.shape[0]
    where = jnp.stack([lax.axis_index(a) for a in ("x", "y", "zl", "core")]).astype(jnp.int32)
    place, blocks = tables(tile_row, tile_column)
    own = weight_tiles
    left, right = turn(own, "x", 1), turn(own, "x", 3)
    beside = swap(own, "zl", 1)
    others = swap(features, "core", 1)
    own_other = swap(own, "core", 1)
    left, right, beside, others, own_other, place, blocks = lax.optimization_barrier(
        (left, right, beside, others, own_other, place, blocks)
    )
    features_near, grad_near, whole = pl.pallas_call(
        load_kernel,
        out_shape=[
            pltpu.VMEM(features.shape, bf16),
            pltpu.VMEM(features.shape, bf16),
            pltpu.VMEM((256, SIDE, SIDE), bf16),
        ],
        in_specs=[SMEM] + [ANY] * (2 + len(FIRST)),
        out_specs=[VMEM] * 3,
        scratch_shapes=[pltpu.SemaphoreType.DMA((len(FIRST) + 2,))],
        compiler_params=PARAMS,
    )(
        where,
        *(stored(v) for v in (features, grad_out, own, left, right, beside, own_other)),
    )
    second = [turn(left, Z, 1), turn(right, Z, 7), turn(left[:8], "x", 1), turn(right[8:], "x", 3)]
    crossed = [swap(left, "core", 1)]
    second, crossed, whole, right, beside = lax.optimization_barrier(
        (second, crossed, whole, right, beside)
    )
    far = second[2:]
    beside_far = (turn(far[0], Z, 1), turn(far[1], Z, 7))
    both_far = jnp.concatenate(far, axis=0)
    crossed += [swap(piece, "core", 1) for piece in (right, beside, both_far)]
    whole = pl.pallas_call(
        more_kernel,
        out_shape=pltpu.VMEM((256, SIDE, SIDE), bf16),
        in_specs=[SMEM, VMEM] + [ANY] * len(MIDDLE),
        out_specs=VMEM,
        scratch_shapes=[pltpu.SemaphoreType.DMA((len(MIDDLE),))],
        input_output_aliases={1: 0},
        compiler_params=PARAMS,
    )(where, near(whole), *(stored(piece) for piece in (*second, *crossed)))
    *beside_far, whole = lax.optimization_barrier((*beside_far, whole))
    crossed = [swap(piece, "core", 1) for piece in (*second[:2], *beside_far)]
    late = [stored(piece) for piece in (*beside_far, *crossed)]
    slopes, whole = pl.pallas_call(
        forward_kernel,
        out_shape=[
            pltpu.VMEM((64, rows_here, SIDE), bf16),
            pltpu.VMEM((256, SIDE, SIDE), bf16),
        ],
        in_specs=[SMEM] * 3 + [VMEM] * 3 + [ANY] * len(LAST),
        out_specs=[VMEM, VMEM],
        scratch_shapes=[pltpu.SemaphoreType.DMA((len(LAST),))],
        input_output_aliases={5: 1},
        compiler_params=PARAMS,
    )(where, place, blocks, near(features_near), near(grad_near), near(whole), *late)
    slopes, others = lax.optimization_barrier((slopes, others))
    other_slopes = swap(slopes, "core", 1)
    xt = pl.pallas_call(
        transpose_kernel,
        out_shape=pltpu.VMEM((64, SIDE, 2 * rows_here), bf16),
        in_specs=[VMEM, VMEM],
        out_specs=VMEM,
        compiler_params=PARAMS,
    )(near(features_near), near(others))
    operands = (tile_row, tile_column, where, near(xt), near(slopes), near(other_slopes))
    sent = pl.pallas_call(
        functools.partial(partial_kernel, SENT, False),
        out_shape=[shape((16, SIDE, SIDE), bf16)] * 4,
        in_specs=[SMEM] * 3 + [VMEM] * 3,
        out_specs=[VMEM] * 4,
        compiler_params=PARAMS,
    )(*operands)
    got = [
        swap(value, axis, (1, 3)[half]) for value, (axis, half) in zip(sent, GROUPS, strict=True)
    ]
    kept = pl.pallas_call(
        functools.partial(partial_kernel, KEPT, True),
        out_shape=[shape((8, SIDE, SIDE), f32)] * 8,
        in_specs=[SMEM] * 3 + [VMEM] * 3,
        out_specs=[VMEM] * 8,
        compiler_params=PARAMS,
    )(*operands)
    kept = list(kept)
    after, kept[0] = lax.optimization_barrier((place, kept[0]))
    backward = functools.partial(
        pl.pallas_call,
        out_shape=shape(features.shape, bf16),
        out_specs=ANY,
        scratch_shapes=[
            pltpu.VMEM((32, rows_here, SIDE), bf16),
            pltpu.SemaphoreType.DMA((32,)),
        ],
        compiler_params=PARAMS,
    )
    grad_features = backward(
        functools.partial(backward_kernel, 0), in_specs=[SMEM] * 2 + [VMEM] * 3
    )(after, blocks, near(grad_near), near(whole), near(slopes))
    got, kept, grad_features = lax.optimization_barrier((got, kept, grad_features))
    grad_features = backward(
        functools.partial(backward_kernel, 1),
        in_specs=[SMEM] * 2 + [VMEM] * 3 + [ANY],
        input_output_aliases={5: 0},
    )(place, blocks, near(grad_near), near(whole), near(slopes), grad_features)

    second = [
        swap((kept[2 * i + 1] + got[i][8:].astype(f32)).astype(bf16), axis, (3, 1)[half])
        for i, (axis, half) in enumerate(GROUPS)
    ]
    held = [
        kept[2 * i] + got[i][:8].astype(f32) + second[i].astype(f32) for i in range(4)
    ]
    rest = [
        jnp.concatenate(
            [held[i].reshape(4, 2, SIDE, SIDE), held[i + 1].reshape(4, 2, SIDE, SIDE)], axis=1
        )
        for i in (0, 2)
    ]
    def reduce_last(parts, axis):
        away = [swap(parts[r].astype(bf16), axis, r).astype(f32) for r in (1, 2, 3)]
        return parts[0] + (away[0] + away[2]) + away[1]

    sums = [reduce_last(rest[0], "y")]
    sums[0], rest[1] = lax.optimization_barrier((sums[0], rest[1]))
    sums.append(reduce_last(rest[1], "x"))
    mine = (sums[1] + swap(sums[0], "zl", 1)).astype(bf16)
    group = pl.pallas_call(
        normalize_kernel,
        out_shape=shape((4, SIDE, SIDE), bf16),
        in_specs=[VMEM] * 4,
        out_specs=VMEM,
        compiler_params=PARAMS,
    )(mine, *(swap(mine, "zh", r) for r in (1, 2, 3)))
    tile_update = pl.pallas_call(
        finish_kernel,
        out_shape=shape((16, SIDE, SIDE), f32),
        in_specs=[SMEM] + [VMEM] * 4,
        out_specs=VMEM,
        compiler_params=PARAMS,
    )(where, group, *(swap(group, "y", r) for r in (1, 2, 3)))
    return grad_features, tile_update


def solution(mesh):
    grid = Mesh(mesh.devices.reshape(SIZES), AXES)
    return jax.shard_map(
        on_device,
        mesh=grid,
        in_specs=(P(AXES, None), P(AXES, None), P(("x", "zl", "core"), None, None), P(), P()),
        out_specs=(P(AXES, None), P(("x", "zl", "core"), None, None)),
        check_vma=False,
    )
```

```python
import functools
import math

import jax
import jax.numpy as jnp
from jax import lax
from jax.experimental import pallas as pl
from jax.experimental.pallas import tpu as pltpu
from jax.sharding import Mesh
from jax.sharding import PartitionSpec as P

AXES = ("zh", "y", "x", "zl", "core")
SIZES = (4, 4, 4, 2, 2)
SIDE = 128
ROOT = math.sqrt(2.0 / math.pi)
CUBIC = 0.044715
UNROLL = 4

VMEM = pl.BlockSpec(memory_space=pltpu.VMEM)
SMEM = pl.BlockSpec(memory_space=pltpu.SMEM)
ANY = pl.BlockSpec(memory_space=pl.ANY)
Z = ("zh", "zl")
PARAMS = pltpu.CompilerParams(vmem_limit_bytes=8 * 1024 * 1024)


def shape(dims, dtype):
    return jax.ShapeDtypeStruct(dims, dtype)


def near(value):
    return pltpu.with_memory_space_constraint(value, pltpu.VMEM)


def stored(value):
    return pltpu.with_memory_space_constraint(value, pltpu.HBM)


def lanes(block):
    return pl.ds(pl.multiple_of(block * SIDE, SIDE), SIDE)


def slope_times(value, cotangent):
    square = value * value
    hyper = jnp.tanh(value * (ROOT + (ROOT * CUBIC) * square))
    slope = 0.5 * (1.0 + hyper) + (0.5 * value) * (1.0 - hyper * hyper) * (
        ROOT + (3.0 * ROOT * CUBIC) * square
    )
    return cotangent * slope


ROUNDS = (
    (0, 0, 0, 16),
    (3, 0, 0, 16),
    (1, 0, 0, 16),
    (0, 1, 0, 16),
    (3, 1, 0, 16),
    (1, 1, 0, 16),
    (2, 0, 0, 8),
    (2, 0, 8, 8),
    (2, 1, 0, 8),
    (2, 1, 8, 8),
)
FIRST = tuple((*ROUNDS[i][:2], 0, *ROUNDS[i][2:]) for i in range(4)) + ((0, 0, 1, 0, 16),)
MIDDLE = (
    *((*ROUNDS[i][:2], 0, *ROUNDS[i][2:]) for i in range(4, 8)),
    *((*ROUNDS[i][:2], 1, *ROUNDS[i][2:]) for i in range(1, 4)),
    (2, 0, 1, 0, 16),
)
LAST = (
    *((*ROUNDS[i][:2], 0, *ROUNDS[i][2:]) for i in (8, 9)),
    *((*ROUNDS[i][:2], 1, *ROUNDS[i][2:]) for i in (4, 5, 8, 9)),
)


def place_copies(where, listed, pieces, w_ref, sems):
    copies = []
    for i, (x, zl, core, first, size) in enumerate(listed):
        owner = (lax.rem(where[0] + x, 4) * 2 + (where[2] ^ zl)) * 2 + (where[3] ^ core)
        to = w_ref.at[pl.ds(owner * 16 + first, size)]
        copies.append(pltpu.make_async_copy(pieces[i], to, sems.at[i]))
    return copies


def run(copies):
    for copy in copies:
        copy.start()
    for copy in copies:
        copy.wait()


def halves_kernel(left, right, low, high, sems):
    run(
        [
            pltpu.make_async_copy(left.at[pl.ds(0, 8)], low, sems.at[0]),
            pltpu.make_async_copy(right.at[pl.ds(8, 8)], high, sems.at[1]),
        ]
    )


def load_kernel(where, x_hbm, g_hbm, *refs):
    pieces, (x_ref, g_ref, w_ref, sems) = refs[: len(FIRST)], refs[len(FIRST) :]
    copies = place_copies(where, FIRST, pieces, w_ref, sems)
    copies.append(pltpu.make_async_copy(x_hbm, x_ref, sems.at[len(FIRST)]))
    copies.append(pltpu.make_async_copy(g_hbm, g_ref, sems.at[len(FIRST) + 1]))
    run(copies)


def more_kernel(where, given, *refs):
    del given
    pieces, (w_ref, sems) = refs[: len(MIDDLE)], refs[len(MIDDLE) :]
    run(place_copies(where, MIDDLE, pieces, w_ref, sems))


def forward_kernel(where, place, blocks, x_ref, g_ref, given, *refs):
    del given
    pieces, (s_ref, w_ref, sems) = refs[: len(LAST)], refs[len(LAST) :]
    run(place_copies(where, LAST, pieces, w_ref, sems))

    def one(group):
        ids = [blocks[group * 4 + m] for m in range(4)]
        x = jnp.concatenate([x_ref[:, lanes(b)] for b in ids], axis=1)
        for first in (0, 2):
            pair = (first, first + 1)
            w = jnp.concatenate(
                [
                    jnp.concatenate([w_ref[place[ids[n] * 4 + (n ^ m)]] for n in pair], axis=1)
                    for m in range(4)
                ],
                axis=0,
            )
            pre = jnp.dot(x, w, preferred_element_type=jnp.float32)
            for k, n in enumerate(pair):
                cot = g_ref[:, lanes(ids[n])].astype(jnp.float32)
                out = slope_times(pre[:, k * SIDE : (k + 1) * SIDE], cot)
                s_ref[ids[n]] = out.astype(jnp.bfloat16)

    def some(step, carry):
        for k in range(UNROLL):
            one(step * UNROLL + k)
        return carry

    lax.fori_loop(0, 16 // UNROLL, some, 0)


def backward_kernel(half, place, blocks, g_ref, w_ref, s_ref, *refs):
    o_hbm, out, sems = refs[-3:]

    def write(at, column):
        return pltpu.make_async_copy(out.at[at], o_hbm.at[:, lanes(column)], sems.at[at])

    def one(step, carry):
        ids = [blocks[(half * 8 + step) * 4 + m] for m in range(4)]
        s = jnp.concatenate([s_ref[b] for b in ids], axis=1)
        for first in (0, 2):
            pair = (first, first + 1)
            w = jnp.concatenate(
                [
                    jnp.concatenate(
                        [w_ref[place[ids[n] * 4 + (n ^ m)]] for n in range(4)], axis=1
                    )
                    for m in pair
                ],
                axis=0,
            )
            back = lax.dot_general(
                s, w, (((1,), (1,)), ((), ())), preferred_element_type=jnp.float32
            )
            for k, m in enumerate(pair):
                cot = g_ref[:, lanes(ids[m])].astype(jnp.float32)
                total = cot + back[:, k * SIDE : (k + 1) * SIDE]
                out[step * 4 + m] = total.astype(jnp.bfloat16)
        for m in range(4):
            write(step * 4 + m, ids[m]).start()
        return carry

    def done(at, carry):
        write(at, blocks[half * 32 + at]).wait()
        return carry

    lax.fori_loop(0, 8, one, 0)
    lax.fori_loop(0, 32, done, 0)


def transpose_kernel(mine_ref, other_ref, xt_ref):
    def one(block, carry):
        rows = jnp.concatenate([mine_ref[:, lanes(block)], other_ref[:, lanes(block)]], axis=0)
        xt_ref[block] = rows.T
        return carry

    lax.fori_loop(0, 64, one, 0)


GROUPS = (("x", 0), ("x", 1), ("y", 0), ("y", 1))
SENT = ((1, 2), (3, 2))
KEPT = ((0, 3), (0, 1))


def partial_kernel(which, splits, rows, cols, where, xt_ref, s_ref, t_ref, *outs):
    x, y, zl, core = where[0], where[1], where[2], where[3]
    for group, (axis, half) in enumerate(GROUPS):
        for p, rel in enumerate(which[half]):
            for other in range(4):
                for low in range(2):
                    rx, ry = (rel, other) if axis == "x" else (other, rel)
                    to_zl = (1 - zl) if axis == "x" else zl
                    k = (y ^ ry) * 4 + half * 2 + low
                    tile = (((x ^ rx) * 2 + to_zl) * 2 + core) * 16 + k
                    row, col = rows[tile], cols[tile]
                    s = jnp.concatenate([s_ref[row], t_ref[row]], axis=0)
                    value = jnp.dot(xt_ref[col], s, preferred_element_type=jnp.float32)
                    if splits:
                        out, at = outs[group * 2 + p], other * 2 + low
                    else:
                        out, at = outs[group], p * 8 + other * 2 + low
                    out[at] = value.astype(out.dtype)


def normalize_kernel(a, b, c, d, out):
    f32 = jnp.float32
    for k in range(4):
        grad = (a[k].astype(f32) + b[k].astype(f32)) + (c[k].astype(f32) + d[k].astype(f32))
        mean = jnp.mean(grad * grad)
        out[k] = (grad * lax.rsqrt(mean + 1e-06)).astype(jnp.bfloat16)


def finish_kernel(where, *refs):
    for r in range(4):
        for k in range(4):
            refs[-1][(where[1] ^ r) * 4 + k] = refs[r][k].astype(jnp.float32)


def swap(value, axis, mask):
    size = SIZES[AXES.index(axis)]
    return lax.ppermute(value, axis, [(i, i ^ mask) for i in range(size)])


def turn(value, axes, by):
    names = axes if isinstance(axes, tuple) else (axes,)
    size = math.prod(SIZES[AXES.index(name)] for name in names)
    return lax.ppermute(value, axes, [(i, (i + by) % size) for i in range(size)])


def tables(tile_row, tile_column):
    differ = tile_row ^ tile_column
    both = lax.reduce(differ, jnp.int32(0), lax.bitwise_or, (0,))
    low = both & -both
    high = both ^ low
    kind = jnp.where((differ & low) != 0, 1, 0) + jnp.where((differ & high) != 0, 2, 0)
    slot = tile_row * 4 + kind
    index = jnp.arange(256, dtype=jnp.int32)
    place = jnp.sum(jnp.where(slot[None, :] == index[:, None], index[None, :], 0), axis=1)
    group = jnp.arange(16, dtype=jnp.int32)
    base = group + (group & ~(low - 1))
    base = base + (base & ~(high - 1))
    member = jnp.stack([0 * low, low, high, both])
    blocks = (base[:, None] ^ member[None, :]).reshape(64)
    return place.astype(jnp.int32), blocks.astype(jnp.int32)


def on_device(features, grad_out, weight_tiles, tile_row, tile_column):
    bf16, f32 = jnp.bfloat16, jnp.float32
    tile_row = tile_row.astype(jnp.int32)
    tile_column = tile_column.astype(jnp.int32)
    rows_here = features.shape[0]
    where = jnp.stack([lax.axis_index(a) for a in ("x", "y", "zl", "core")]).astype(jnp.int32)
    place, blocks = tables(tile_row, tile_column)
    own = weight_tiles
    left, right = turn(own, "x", 1), turn(own, "x", 3)
    beside = swap(own, "zl", 1)
    others = swap(features, "core", 1)
    own_other = swap(own, "core", 1)
    left, right, beside, others, own_other, place, blocks = lax.optimization_barrier(
        (left, right, beside, others, own_other, place, blocks)
    )
    features_near, grad_near, whole = pl.pallas_call(
        load_kernel,
        out_shape=[
            pltpu.VMEM(features.shape, bf16),
            pltpu.VMEM(features.shape, bf16),
            pltpu.VMEM((256, SIDE, SIDE), bf16),
        ],
        in_specs=[SMEM] + [ANY] * (2 + len(FIRST)),
        out_specs=[VMEM] * 3,
        scratch_shapes=[pltpu.SemaphoreType.DMA((len(FIRST) + 2,))],
        compiler_params=PARAMS,
    )(
        where,
        *(stored(v) for v in (features, grad_out, own)),
        *(near(v) for v in (left, right, beside, own_other)),
    )
    low, high = pl.pallas_call(
        halves_kernel,
        out_shape=[pltpu.VMEM((8, SIDE, SIDE), bf16)] * 2,
        in_specs=[ANY] * 2,
        out_specs=[VMEM] * 2,
        scratch_shapes=[pltpu.SemaphoreType.DMA((2,))],
        compiler_params=PARAMS,
    )(near(left), near(right))
    second = [turn(left, Z, 1), turn(right, Z, 7), turn(low, "x", 1), turn(high, "x", 3)]
    crossed = [swap(left, "core", 1)]
    second, crossed, whole, right, beside = lax.optimization_barrier(
        (second, crossed, whole, right, beside)
    )
    far = second[2:]
    beside_far = (turn(far[0], Z, 1), turn(far[1], Z, 7))
    both_far = jnp.concatenate(far, axis=0)
    crossed += [swap(piece, "core", 1) for piece in (right, beside, both_far)]
    whole = pl.pallas_call(
        more_kernel,
        out_shape=pltpu.VMEM((256, SIDE, SIDE), bf16),
        in_specs=[SMEM, VMEM] + [ANY] * len(MIDDLE),
        out_specs=VMEM,
        scratch_shapes=[pltpu.SemaphoreType.DMA((len(MIDDLE),))],
        input_output_aliases={1: 0},
        compiler_params=PARAMS,
    )(where, near(whole), *(near(piece) for piece in (*second, *crossed)))
    *beside_far, whole = lax.optimization_barrier((*beside_far, whole))
    crossed = [swap(piece, "core", 1) for piece in (*second[:2], *beside_far)]
    late = [near(piece) for piece in (*beside_far, *crossed)]
    slopes, whole = pl.pallas_call(
        forward_kernel,
        out_shape=[
            pltpu.VMEM((64, rows_here, SIDE), bf16),
            pltpu.VMEM((256, SIDE, SIDE), bf16),
        ],
        in_specs=[SMEM] * 3 + [VMEM] * 3 + [ANY] * len(LAST),
        out_specs=[VMEM, VMEM],
        scratch_shapes=[pltpu.SemaphoreType.DMA((len(LAST),))],
        input_output_aliases={5: 1},
        compiler_params=PARAMS,
    )(where, place, blocks, near(features_near), near(grad_near), near(whole), *late)
    slopes, others = lax.optimization_barrier((slopes, others))
    other_slopes = swap(slopes, "core", 1)
    xt = pl.pallas_call(
        transpose_kernel,
        out_shape=pltpu.VMEM((64, SIDE, 2 * rows_here), bf16),
        in_specs=[VMEM, VMEM],
        out_specs=VMEM,
        compiler_params=PARAMS,
    )(near(features_near), near(others))
    operands = (tile_row, tile_column, where, near(xt), near(slopes), near(other_slopes))
    sent = pl.pallas_call(
        functools.partial(partial_kernel, SENT, False),
        out_shape=[shape((16, SIDE, SIDE), bf16)] * 4,
        in_specs=[SMEM] * 3 + [VMEM] * 3,
        out_specs=[VMEM] * 4,
        compiler_params=PARAMS,
    )(*operands)
    got = [
        swap(value, axis, (1, 3)[half]) for value, (axis, half) in zip(sent, GROUPS, strict=True)
    ]
    kept = pl.pallas_call(
        functools.partial(partial_kernel, KEPT, True),
        out_shape=[shape((8, SIDE, SIDE), f32)] * 8,
        in_specs=[SMEM] * 3 + [VMEM] * 3,
        out_specs=[VMEM] * 8,
        compiler_params=PARAMS,
    )(*operands)
    kept = list(kept)
    after, kept[0] = lax.optimization_barrier((place, kept[0]))
    backward = functools.partial(
        pl.pallas_call,
        out_shape=shape(features.shape, bf16),
        out_specs=ANY,
        scratch_shapes=[
            pltpu.VMEM((32, rows_here, SIDE), bf16),
            pltpu.SemaphoreType.DMA((32,)),
        ],
        compiler_params=PARAMS,
    )
    grad_features = backward(
        functools.partial(backward_kernel, 0), in_specs=[SMEM] * 2 + [VMEM] * 3
    )(after, blocks, near(grad_near), near(whole), near(slopes))
    got, kept, grad_features = lax.optimization_barrier((got, kept, grad_features))
    second = [
        swap((kept[2 * i + 1] + got[i][8:].astype(f32)).astype(bf16), axis, (3, 1)[half])
        for i, (axis, half) in enumerate(GROUPS)
    ]
    held = [
        kept[2 * i] + got[i][:8].astype(f32) + second[i].astype(f32) for i in range(4)
    ]
    rest = [
        jnp.concatenate(
            [held[i].reshape(4, 2, SIDE, SIDE), held[i + 1].reshape(4, 2, SIDE, SIDE)], axis=1
        )
        for i in (0, 2)
    ]
    def reduce_last(parts, axis):
        away = [swap(parts[r].astype(bf16), axis, r).astype(f32) for r in (1, 2, 3)]
        return parts[0] + (away[0] + away[2]) + away[1]

    sums = [reduce_last(rest[0], "y")]
    sums[0], rest[1] = lax.optimization_barrier((sums[0], rest[1]))
    sums.append(reduce_last(rest[1], "x"))
    mine = (sums[1] + swap(sums[0], "zl", 1)).astype(bf16)
    place, mine = lax.optimization_barrier((place, mine))
    grad_features = backward(
        functools.partial(backward_kernel, 1),
        in_specs=[SMEM] * 2 + [VMEM] * 3 + [ANY],
        input_output_aliases={5: 0},
    )(place, blocks, near(grad_near), near(whole), near(slopes), grad_features)
    across = [swap(mine, "zh", r) for r in (1, 2, 3)]
    across, grad_features = lax.optimization_barrier((across, grad_features))
    group = pl.pallas_call(
        normalize_kernel,
        out_shape=shape((4, SIDE, SIDE), bf16),
        in_specs=[VMEM] * 4,
        out_specs=VMEM,
        compiler_params=PARAMS,
    )(mine, *across)
    tile_update = pl.pallas_call(
        finish_kernel,
        out_shape=shape((16, SIDE, SIDE), f32),
        in_specs=[SMEM] + [VMEM] * 4,
        out_specs=VMEM,
        compiler_params=PARAMS,
    )(where, group, *(swap(group, "y", r) for r in (1, 2, 3)))
    return grad_features, tile_update


def solution(mesh):
    grid = Mesh(mesh.devices.reshape(SIZES), AXES)
    return jax.shard_map(
        on_device,
        mesh=grid,
        in_specs=(P(AXES, None), P(AXES, None), P(("x", "zl", "core"), None, None), P(), P()),
        out_specs=(P(AXES, None), P(("x", "zl", "core"), None, None)),
        check_vma=False,
    )
```

```python
import functools
import math

import jax
import jax.numpy as jnp
from jax import lax
from jax.experimental import pallas as pl
from jax.experimental.pallas import tpu as pltpu
from jax.sharding import Mesh
from jax.sharding import PartitionSpec as P

AXES = ("zh", "y", "x", "zl", "core")
SIZES = (4, 4, 4, 2, 2)
SIDE = 128
ROOT = math.sqrt(2.0 / math.pi)
CUBIC = 0.044715
UNROLL = 4

VMEM = pl.BlockSpec(memory_space=pltpu.VMEM)
SMEM = pl.BlockSpec(memory_space=pltpu.SMEM)
ANY = pl.BlockSpec(memory_space=pl.ANY)
Z = ("zh", "zl")
PARAMS = pltpu.CompilerParams(vmem_limit_bytes=8 * 1024 * 1024)


def shape(dims, dtype):
    return jax.ShapeDtypeStruct(dims, dtype)


def near(value):
    return pltpu.with_memory_space_constraint(value, pltpu.VMEM)


def stored(value):
    return pltpu.with_memory_space_constraint(value, pltpu.HBM)


def lanes(block):
    return pl.ds(pl.multiple_of(block * SIDE, SIDE), SIDE)


def slope_times(value, cotangent):
    square = value * value
    hyper = jnp.tanh(value * (ROOT + (ROOT * CUBIC) * square))
    slope = 0.5 * (1.0 + hyper) + (0.5 * value) * (1.0 - hyper * hyper) * (
        ROOT + (3.0 * ROOT * CUBIC) * square
    )
    return cotangent * slope


ROUNDS = (
    (0, 0, 0, 16),
    (1, 0, 0, 16),
    (3, 0, 0, 16),
    (0, 1, 0, 16),
    (1, 1, 0, 16),
    (3, 1, 0, 16),
    (2, 0, 0, 8),
    (2, 0, 8, 8),
    (2, 1, 0, 8),
    (2, 1, 8, 8),
)
FIRST = tuple((*ROUNDS[i][:2], 0, *ROUNDS[i][2:]) for i in range(4)) + ((0, 0, 1, 0, 16),)
MIDDLE = (
    *((*ROUNDS[i][:2], 0, *ROUNDS[i][2:]) for i in range(4, 8)),
    *((*ROUNDS[i][:2], 1, *ROUNDS[i][2:]) for i in range(1, 5)),
)
LAST = (
    *((*ROUNDS[i][:2], 0, *ROUNDS[i][2:]) for i in (8, 9)),
    *((*ROUNDS[i][:2], 1, *ROUNDS[i][2:]) for i in (5, 8, 9)),
    (2, 0, 1, 0, 16),
)


def place_copies(where, listed, pieces, w_ref, sems):
    copies = []
    for i, (x, zl, core, first, size) in enumerate(listed):
        owner = ((where[0] ^ x) * 2 + (where[2] ^ zl)) * 2 + (where[3] ^ core)
        to = w_ref.at[pl.ds(owner * 16 + first, size)]
        copies.append(pltpu.make_async_copy(pieces[i], to, sems.at[i]))
    return copies


def run(copies):
    for copy in copies:
        copy.start()
    for copy in copies:
        copy.wait()


def halves_kernel(left, right, low, high, sems):
    run(
        [
            pltpu.make_async_copy(left.at[pl.ds(0, 8)], low, sems.at[0]),
            pltpu.make_async_copy(right.at[pl.ds(8, 8)], high, sems.at[1]),
        ]
    )


def load_kernel(where, x_hbm, g_hbm, *refs):
    pieces, (x_ref, g_ref, w_ref, sems) = refs[: len(FIRST)], refs[len(FIRST) :]
    copies = place_copies(where, FIRST, pieces, w_ref, sems)
    copies.append(pltpu.make_async_copy(x_hbm, x_ref, sems.at[len(FIRST)]))
    copies.append(pltpu.make_async_copy(g_hbm, g_ref, sems.at[len(FIRST) + 1]))
    run(copies)


def more_kernel(where, given, *refs):
    del given
    pieces, (w_ref, sems) = refs[: len(MIDDLE)], refs[len(MIDDLE) :]
    run(place_copies(where, MIDDLE, pieces, w_ref, sems))


def forward_kernel(where, place, blocks, x_ref, g_ref, given, *refs):
    del given
    pieces, (s_ref, w_ref, sems) = refs[: len(LAST)], refs[len(LAST) :]
    run(place_copies(where, LAST, pieces, w_ref, sems))

    def one(group):
        ids = [blocks[group * 4 + m] for m in range(4)]
        x = jnp.concatenate([x_ref[:, lanes(b)] for b in ids], axis=1)
        for first in (0, 2):
            pair = (first, first + 1)
            w = jnp.concatenate(
                [
                    jnp.concatenate([w_ref[place[ids[n] * 4 + (n ^ m)]] for n in pair], axis=1)
                    for m in range(4)
                ],
                axis=0,
            )
            pre = jnp.dot(x, w, preferred_element_type=jnp.float32)
            for k, n in enumerate(pair):
                cot = g_ref[:, lanes(ids[n])].astype(jnp.float32)
                out = slope_times(pre[:, k * SIDE : (k + 1) * SIDE], cot)
                s_ref[ids[n]] = out.astype(jnp.bfloat16)

    def some(step, carry):
        for k in range(UNROLL):
            one(step * UNROLL + k)
        return carry

    lax.fori_loop(0, 16 // UNROLL, some, 0)


def backward_kernel(half, place, blocks, g_ref, w_ref, s_ref, *refs):
    o_hbm, out, sems = refs[-3:]

    def write(at, column):
        return pltpu.make_async_copy(out.at[at], o_hbm.at[:, lanes(column)], sems.at[at])

    def one(step, carry):
        ids = [blocks[(half * 8 + step) * 4 + m] for m in range(4)]
        s = jnp.concatenate([s_ref[b] for b in ids], axis=1)
        for first in (0, 2):
            pair = (first, first + 1)
            w = jnp.concatenate(
                [
                    jnp.concatenate(
                        [w_ref[place[ids[n] * 4 + (n ^ m)]] for n in range(4)], axis=1
                    )
                    for m in pair
                ],
                axis=0,
            )
            back = lax.dot_general(
                s, w, (((1,), (1,)), ((), ())), preferred_element_type=jnp.float32
            )
            for k, m in enumerate(pair):
                cot = g_ref[:, lanes(ids[m])].astype(jnp.float32)
                total = cot + back[:, k * SIDE : (k + 1) * SIDE]
                out[step * 4 + m] = total.astype(jnp.bfloat16)
        for m in range(4):
            write(step * 4 + m, ids[m]).start()
        return carry

    def done(at, carry):
        write(at, blocks[half * 32 + at]).wait()
        return carry

    lax.fori_loop(0, 8, one, 0)
    lax.fori_loop(0, 32, done, 0)


def transpose_kernel(mine_ref, other_ref, xt_ref):
    def one(block, carry):
        rows = jnp.concatenate([mine_ref[:, lanes(block)], other_ref[:, lanes(block)]], axis=0)
        xt_ref[block] = rows.T
        return carry

    lax.fori_loop(0, 64, one, 0)


GROUPS = (("x", 0), ("x", 1), ("y", 0), ("y", 1))
SENT = ((1, 2), (3, 2))
KEPT = ((0, 3), (0, 1))


def partial_kernel(which, splits, rows, cols, where, xt_ref, s_ref, t_ref, *outs):
    x, y, zl, core = where[0], where[1], where[2], where[3]
    for group, (axis, half) in enumerate(GROUPS):
        for p, rel in enumerate(which[half]):
            for other in range(4):
                for low in range(2):
                    rx, ry = (rel, other) if axis == "x" else (other, rel)
                    to_zl = (1 - zl) if axis == "x" else zl
                    k = (y ^ ry) * 4 + half * 2 + low
                    tile = (((x ^ rx) * 2 + to_zl) * 2 + core) * 16 + k
                    row, col = rows[tile], cols[tile]
                    s = jnp.concatenate([s_ref[row], t_ref[row]], axis=0)
                    value = jnp.dot(xt_ref[col], s, preferred_element_type=jnp.float32)
                    if splits:
                        out, at = outs[group * 2 + p], other * 2 + low
                    else:
                        out, at = outs[group], p * 8 + other * 2 + low
                    out[at] = value.astype(out.dtype)


def normalize_kernel(a, b, c, d, out):
    f32 = jnp.float32
    for k in range(4):
        grad = (a[k].astype(f32) + b[k].astype(f32)) + (c[k].astype(f32) + d[k].astype(f32))
        mean = jnp.mean(grad * grad)
        out[k] = (grad * lax.rsqrt(mean + 1e-06)).astype(jnp.bfloat16)


def finish_kernel(where, *refs):
    for r in range(4):
        for k in range(4):
            refs[-1][(where[1] ^ r) * 4 + k] = refs[r][k].astype(jnp.float32)


def swap(value, axis, mask):
    size = SIZES[AXES.index(axis)]
    return lax.ppermute(value, axis, [(i, i ^ mask) for i in range(size)])


def cross(value):
    return lax.ppermute(
        value, Z, [(z, (z + 1) % 8 if z % 2 else (z - 1) % 8) for z in range(8)]
    )


def tables(tile_row, tile_column):
    differ = tile_row ^ tile_column
    both = lax.reduce(differ, jnp.int32(0), lax.bitwise_or, (0,))
    low = both & -both
    high = both ^ low
    kind = jnp.where((differ & low) != 0, 1, 0) + jnp.where((differ & high) != 0, 2, 0)
    slot = tile_row * 4 + kind
    index = jnp.arange(256, dtype=jnp.int32)
    place = jnp.sum(jnp.where(slot[None, :] == index[:, None], index[None, :], 0), axis=1)
    group = jnp.arange(16, dtype=jnp.int32)
    base = group + (group & ~(low - 1))
    base = base + (base & ~(high - 1))
    member = jnp.stack([0 * low, low, high, both])
    blocks = (base[:, None] ^ member[None, :]).reshape(64)
    return place.astype(jnp.int32), blocks.astype(jnp.int32)


def on_device(features, grad_out, weight_tiles, tile_row, tile_column):
    bf16, f32 = jnp.bfloat16, jnp.float32
    tile_row = tile_row.astype(jnp.int32)
    tile_column = tile_column.astype(jnp.int32)
    rows_here = features.shape[0]
    where = jnp.stack([lax.axis_index(a) for a in ("x", "y", "zl", "core")]).astype(jnp.int32)
    place, blocks = tables(tile_row, tile_column)
    own = weight_tiles
    left, right = swap(own, "x", 1), swap(own, "x", 3)
    beside = swap(own, "zl", 1)
    others = swap(features, "core", 1)
    own_other = swap(own, "core", 1)
    left, right, beside, others, own_other, place, blocks = lax.optimization_barrier(
        (left, right, beside, others, own_other, place, blocks)
    )
    features_near, grad_near, whole = pl.pallas_call(
        load_kernel,
        out_shape=[
            pltpu.VMEM(features.shape, bf16),
            pltpu.VMEM(features.shape, bf16),
            pltpu.VMEM((256, SIDE, SIDE), bf16),
        ],
        in_specs=[SMEM] + [ANY] * (2 + len(FIRST)),
        out_specs=[VMEM] * 3,
        scratch_shapes=[pltpu.SemaphoreType.DMA((len(FIRST) + 2,))],
        compiler_params=PARAMS,
    )(
        where,
        *(stored(v) for v in (features, grad_out, own)),
        *(near(v) for v in (left, right, beside, own_other)),
    )
    low, high = pl.pallas_call(
        halves_kernel,
        out_shape=[pltpu.VMEM((8, SIDE, SIDE), bf16)] * 2,
        in_specs=[ANY] * 2,
        out_specs=[VMEM] * 2,
        scratch_shapes=[pltpu.SemaphoreType.DMA((2,))],
        compiler_params=PARAMS,
    )(near(left), near(right))
    second = [swap(left, "zl", 1), cross(right), swap(low, "x", 3), swap(high, "x", 1)]
    crossed = [swap(left, "core", 1)]
    second, crossed, whole, right, beside = lax.optimization_barrier(
        (second, crossed, whole, right, beside)
    )
    far = second[2:]
    beside_far = (swap(far[0], "zl", 1), cross(far[1]))
    both_far = jnp.concatenate(far, axis=0)
    crossed += [swap(piece, "core", 1) for piece in (right, beside, second[0])]
    whole = pl.pallas_call(
        more_kernel,
        out_shape=pltpu.VMEM((256, SIDE, SIDE), bf16),
        in_specs=[SMEM, VMEM] + [ANY] * len(MIDDLE),
        out_specs=VMEM,
        scratch_shapes=[pltpu.SemaphoreType.DMA((len(MIDDLE),))],
        input_output_aliases={1: 0},
        compiler_params=PARAMS,
    )(where, near(whole), *(near(piece) for piece in (*second, *crossed)))
    *beside_far, whole, both_far = lax.optimization_barrier((*beside_far, whole, both_far))
    crossed = [swap(piece, "core", 1) for piece in (second[1], *beside_far, both_far)]
    late = [near(piece) for piece in (*beside_far, *crossed)]
    slopes, whole = pl.pallas_call(
        forward_kernel,
        out_shape=[
            pltpu.VMEM((64, rows_here, SIDE), bf16),
            pltpu.VMEM((256, SIDE, SIDE), bf16),
        ],
        in_specs=[SMEM] * 3 + [VMEM] * 3 + [ANY] * len(LAST),
        out_specs=[VMEM, VMEM],
        scratch_shapes=[pltpu.SemaphoreType.DMA((len(LAST),))],
        input_output_aliases={5: 1},
        compiler_params=PARAMS,
    )(where, place, blocks, near(features_near), near(grad_near), near(whole), *late)
    slopes, others = lax.optimization_barrier((slopes, others))
    other_slopes = swap(slopes, "core", 1)
    xt = pl.pallas_call(
        transpose_kernel,
        out_shape=pltpu.VMEM((64, SIDE, 2 * rows_here), bf16),
        in_specs=[VMEM, VMEM],
        out_specs=VMEM,
        compiler_params=PARAMS,
    )(near(features_near), near(others))
    operands = (tile_row, tile_column, where, near(xt), near(slopes), near(other_slopes))
    sent = pl.pallas_call(
        functools.partial(partial_kernel, SENT, False),
        out_shape=[shape((16, SIDE, SIDE), bf16)] * 4,
        in_specs=[SMEM] * 3 + [VMEM] * 3,
        out_specs=[VMEM] * 4,
        compiler_params=PARAMS,
    )(*operands)
    got = [
        swap(value, axis, (1, 3)[half]) for value, (axis, half) in zip(sent, GROUPS, strict=True)
    ]
    kept = pl.pallas_call(
        functools.partial(partial_kernel, KEPT, True),
        out_shape=[shape((8, SIDE, SIDE), f32)] * 8,
        in_specs=[SMEM] * 3 + [VMEM] * 3,
        out_specs=[VMEM] * 8,
        compiler_params=PARAMS,
    )(*operands)
    kept = list(kept)
    after, kept[0] = lax.optimization_barrier((place, kept[0]))
    backward = functools.partial(
        pl.pallas_call,
        out_shape=shape(features.shape, bf16),
        out_specs=ANY,
        scratch_shapes=[
            pltpu.VMEM((32, rows_here, SIDE), bf16),
            pltpu.SemaphoreType.DMA((32,)),
        ],
        compiler_params=PARAMS,
    )
    grad_features = backward(
        functools.partial(backward_kernel, 0), in_specs=[SMEM] * 2 + [VMEM] * 3
    )(after, blocks, near(grad_near), near(whole), near(slopes))
    got, kept, grad_features = lax.optimization_barrier((got, kept, grad_features))
    second = [
        swap((kept[2 * i + 1] + got[i][8:].astype(f32)).astype(bf16), axis, (3, 1)[half])
        for i, (axis, half) in enumerate(GROUPS)
    ]
    held = [
        kept[2 * i] + got[i][:8].astype(f32) + second[i].astype(f32) for i in range(4)
    ]
    rest = [
        jnp.concatenate(
            [held[i].reshape(4, 2, SIDE, SIDE), held[i + 1].reshape(4, 2, SIDE, SIDE)], axis=1
        )
        for i in (0, 2)
    ]
    def reduce_last(parts, axis):
        away = [swap(parts[r].astype(bf16), axis, r).astype(f32) for r in (1, 2, 3)]
        return parts[0] + (away[0] + away[2]) + away[1]

    sums = [reduce_last(rest[0], "y")]
    sums[0], rest[1] = lax.optimization_barrier((sums[0], rest[1]))
    sums.append(reduce_last(rest[1], "x"))
    mine = (sums[1] + swap(sums[0], "zl", 1)).astype(bf16)
    place, mine = lax.optimization_barrier((place, mine))
    grad_features = backward(
        functools.partial(backward_kernel, 1),
        in_specs=[SMEM] * 2 + [VMEM] * 3 + [ANY],
        input_output_aliases={5: 0},
    )(place, blocks, near(grad_near), near(whole), near(slopes), grad_features)
    across = [swap(mine, "zh", r) for r in (1, 2, 3)]
    across, grad_features = lax.optimization_barrier((across, grad_features))
    group = pl.pallas_call(
        normalize_kernel,
        out_shape=shape((4, SIDE, SIDE), bf16),
        in_specs=[VMEM] * 4,
        out_specs=VMEM,
        compiler_params=PARAMS,
    )(mine, *across)
    tile_update = pl.pallas_call(
        finish_kernel,
        out_shape=shape((16, SIDE, SIDE), f32),
        in_specs=[SMEM] + [VMEM] * 4,
        out_specs=VMEM,
        compiler_params=PARAMS,
    )(where, group, *(swap(group, "y", r) for r in (1, 2, 3)))
    return grad_features, tile_update


def solution(mesh):
    grid = Mesh(mesh.devices.reshape(SIZES), AXES)
    return jax.shard_map(
        on_device,
        mesh=grid,
        in_specs=(P(AXES, None), P(AXES, None), P(("x", "zl", "core"), None, None), P(), P()),
        out_specs=(P(AXES, None), P(("x", "zl", "core"), None, None)),
        check_vma=False,
    )
```

```python
import functools
import math

import jax
import jax.numpy as jnp
from jax import lax
from jax.experimental import pallas as pl
from jax.experimental.pallas import tpu as pltpu
from jax.sharding import Mesh
from jax.sharding import PartitionSpec as P

AXES = ("zh", "y", "x", "zl", "core")
SIZES = (4, 4, 4, 2, 2)
SIDE = 128
ROOT = math.sqrt(2.0 / math.pi)
CUBIC = 0.044715
UNROLL = 4

VMEM = pl.BlockSpec(memory_space=pltpu.VMEM)
SMEM = pl.BlockSpec(memory_space=pltpu.SMEM)
ANY = pl.BlockSpec(memory_space=pl.ANY)
Z = ("zh", "zl")
PARAMS = pltpu.CompilerParams(vmem_limit_bytes=8 * 1024 * 1024)


def shape(dims, dtype):
    return jax.ShapeDtypeStruct(dims, dtype)


def near(value):
    return pltpu.with_memory_space_constraint(value, pltpu.VMEM)


def stored(value):
    return pltpu.with_memory_space_constraint(value, pltpu.HBM)


def lanes(block):
    return pl.ds(pl.multiple_of(block * SIDE, SIDE), SIDE)


def slope_times(value, cotangent):
    square = value * value
    hyper = jnp.tanh(value * (ROOT + (ROOT * CUBIC) * square))
    slope = 0.5 * (1.0 + hyper) + (0.5 * value) * (1.0 - hyper * hyper) * (
        ROOT + (3.0 * ROOT * CUBIC) * square
    )
    return cotangent * slope


ROUNDS = (
    (0, 0, 0, 16),
    (1, 0, 0, 16),
    (3, 0, 0, 16),
    (0, 1, 0, 16),
    (1, 1, 0, 16),
    (3, 1, 0, 16),
    (2, 0, 0, 8),
    (2, 0, 8, 8),
    (2, 1, 0, 8),
    (2, 1, 8, 8),
)
FIRST = tuple((*ROUNDS[i][:2], 0, *ROUNDS[i][2:]) for i in range(4)) + ((0, 0, 1, 0, 16),)
MIDDLE = (
    *((*ROUNDS[i][:2], 0, *ROUNDS[i][2:]) for i in range(4, 8)),
    *((*ROUNDS[i][:2], 1, *ROUNDS[i][2:]) for i in range(1, 5)),
)
LAST = (
    *((*ROUNDS[i][:2], 0, *ROUNDS[i][2:]) for i in (8, 9)),
    *((*ROUNDS[i][:2], 1, *ROUNDS[i][2:]) for i in (5, 8, 9)),
    (2, 0, 1, 0, 16),
)


def place_copies(where, listed, pieces, w_ref, sems):
    copies = []
    for i, (x, zl, core, first, size) in enumerate(listed):
        owner = ((where[0] ^ x) * 2 + (where[2] ^ zl)) * 2 + (where[3] ^ core)
        to = w_ref.at[pl.ds(owner * 16 + first, size)]
        copies.append(pltpu.make_async_copy(pieces[i], to, sems.at[i]))
    return copies


def run(copies):
    for copy in copies:
        copy.start()
    for copy in copies:
        copy.wait()


def halves_kernel(left, right, low, high, sems):
    run(
        [
            pltpu.make_async_copy(left.at[pl.ds(0, 8)], low, sems.at[0]),
            pltpu.make_async_copy(right.at[pl.ds(8, 8)], high, sems.at[1]),
        ]
    )


def load_kernel(where, x_hbm, g_hbm, *refs):
    pieces, (x_ref, g_ref, w_ref, sems) = refs[: len(FIRST)], refs[len(FIRST) :]
    copies = place_copies(where, FIRST, pieces, w_ref, sems)
    copies.append(pltpu.make_async_copy(x_hbm, x_ref, sems.at[len(FIRST)]))
    copies.append(pltpu.make_async_copy(g_hbm, g_ref, sems.at[len(FIRST) + 1]))
    run(copies)


def more_kernel(where, given, *refs):
    del given
    pieces, (w_ref, sems) = refs[: len(MIDDLE)], refs[len(MIDDLE) :]
    run(place_copies(where, MIDDLE, pieces, w_ref, sems))


def forward_kernel(where, place, blocks, x_ref, g_ref, given, *refs):
    del given
    pieces, (s_ref, w_ref, sems) = refs[: len(LAST)], refs[len(LAST) :]
    run(place_copies(where, LAST, pieces, w_ref, sems))

    def one(group):
        ids = [blocks[group * 4 + m] for m in range(4)]
        x = jnp.concatenate([x_ref[:, lanes(b)] for b in ids], axis=1)
        for first in (0, 2):
            pair = (first, first + 1)
            w = jnp.concatenate(
                [
                    jnp.concatenate([w_ref[place[ids[n] * 4 + (n ^ m)]] for n in pair], axis=1)
                    for m in range(4)
                ],
                axis=0,
            )
            pre = jnp.dot(x, w, preferred_element_type=jnp.float32)
            for k, n in enumerate(pair):
                cot = g_ref[:, lanes(ids[n])].astype(jnp.float32)
                out = slope_times(pre[:, k * SIDE : (k + 1) * SIDE], cot)
                s_ref[ids[n]] = out.astype(jnp.bfloat16)

    def some(step, carry):
        for k in range(UNROLL):
            one(step * UNROLL + k)
        return carry

    lax.fori_loop(0, 16 // UNROLL, some, 0)


def backward_kernel(half, place, blocks, g_ref, w_ref, s_ref, *refs):
    o_hbm, out, sems = refs[-3:]

    def write(at, column):
        return pltpu.make_async_copy(out.at[at], o_hbm.at[:, lanes(column)], sems.at[at])

    def one(step, carry):
        ids = [blocks[(half * 8 + step) * 4 + m] for m in range(4)]
        s = jnp.concatenate([s_ref[b] for b in ids], axis=1)
        for first in (0, 2):
            pair = (first, first + 1)
            w = jnp.concatenate(
                [
                    jnp.concatenate(
                        [w_ref[place[ids[n] * 4 + (n ^ m)]] for n in range(4)], axis=1
                    )
                    for m in pair
                ],
                axis=0,
            )
            back = lax.dot_general(
                s, w, (((1,), (1,)), ((), ())), preferred_element_type=jnp.float32
            )
            for k, m in enumerate(pair):
                cot = g_ref[:, lanes(ids[m])].astype(jnp.float32)
                total = cot + back[:, k * SIDE : (k + 1) * SIDE]
                out[step * 4 + m] = total.astype(jnp.bfloat16)
        for m in range(4):
            write(step * 4 + m, ids[m]).start()
        return carry

    def done(at, carry):
        write(at, blocks[half * 32 + at]).wait()
        return carry

    lax.fori_loop(0, 8, one, 0)
    lax.fori_loop(0, 32, done, 0)


def transpose_kernel(mine_ref, other_ref, xt_ref):
    def one(block, carry):
        rows = jnp.concatenate([mine_ref[:, lanes(block)], other_ref[:, lanes(block)]], axis=0)
        xt_ref[block] = rows.T
        return carry

    lax.fori_loop(0, 64, one, 0)


GROUPS = (("x", 0), ("x", 1), ("y", 0), ("y", 1))
SENT = ((1, 2), (3, 2))
KEPT = ((0, 3), (0, 1))


def partial_kernel(which, splits, rows, cols, where, xt_ref, s_ref, t_ref, *outs):
    x, y, zl, core = where[0], where[1], where[2], where[3]
    for group, (axis, half) in enumerate(GROUPS):
        for p, rel in enumerate(which[half]):
            for other in range(4):
                for low in range(2):
                    rx, ry = (rel, other) if axis == "x" else (other, rel)
                    to_zl = (1 - zl) if axis == "x" else zl
                    k = (y ^ ry) * 4 + half * 2 + low
                    tile = (((x ^ rx) * 2 + to_zl) * 2 + core) * 16 + k
                    row, col = rows[tile], cols[tile]
                    s = jnp.concatenate([s_ref[row], t_ref[row]], axis=0)
                    value = jnp.dot(xt_ref[col], s, preferred_element_type=jnp.float32)
                    if splits:
                        out, at = outs[group * 2 + p], other * 2 + low
                    else:
                        out, at = outs[group], p * 8 + other * 2 + low
                    out[at] = value.astype(out.dtype)


def normalize_kernel(a, b, c, d, out):
    f32 = jnp.float32
    for k in range(4):
        grad = (a[k].astype(f32) + b[k].astype(f32)) + (c[k].astype(f32) + d[k].astype(f32))
        mean = jnp.mean(grad * grad)
        out[k] = (grad * lax.rsqrt(mean + 1e-06)).astype(jnp.bfloat16)


def finish_kernel(where, *refs):
    for r in range(4):
        for k in range(4):
            refs[-1][(where[1] ^ r) * 4 + k] = refs[r][k].astype(jnp.float32)


def swap(value, axis, mask):
    size = SIZES[AXES.index(axis)]
    return lax.ppermute(value, axis, [(i, i ^ mask) for i in range(size)])


def cross(value):
    return lax.ppermute(
        value, Z, [(z, (z + 1) % 8 if z % 2 else (z - 1) % 8) for z in range(8)]
    )


def tables(tile_row, tile_column):
    differ = tile_row ^ tile_column
    both = lax.reduce(differ, jnp.int32(0), lax.bitwise_or, (0,))
    low = both & -both
    high = both ^ low
    kind = jnp.where((differ & low) != 0, 1, 0) + jnp.where((differ & high) != 0, 2, 0)
    slot = tile_row * 4 + kind
    index = jnp.arange(256, dtype=jnp.int32)
    place = jnp.sum(jnp.where(slot[None, :] == index[:, None], index[None, :], 0), axis=1)
    group = jnp.arange(16, dtype=jnp.int32)
    base = group + (group & ~(low - 1))
    base = base + (base & ~(high - 1))
    member = jnp.stack([0 * low, low, high, both])
    blocks = (base[:, None] ^ member[None, :]).reshape(64)
    return place.astype(jnp.int32), blocks.astype(jnp.int32)


def on_device(features, grad_out, weight_tiles, tile_row, tile_column):
    bf16, f32 = jnp.bfloat16, jnp.float32
    tile_row = tile_row.astype(jnp.int32)
    tile_column = tile_column.astype(jnp.int32)
    rows_here = features.shape[0]
    where = jnp.stack([lax.axis_index(a) for a in ("x", "y", "zl", "core")]).astype(jnp.int32)
    place, blocks = tables(tile_row, tile_column)
    own = weight_tiles
    left, right = swap(own, "x", 1), swap(own, "x", 3)
    beside = swap(own, "zl", 1)
    others = swap(features, "core", 1)
    own_other = swap(own, "core", 1)
    left, right, beside, others, own_other, place, blocks = lax.optimization_barrier(
        (left, right, beside, others, own_other, place, blocks)
    )
    features_near, grad_near, whole = pl.pallas_call(
        load_kernel,
        out_shape=[
            pltpu.VMEM(features.shape, bf16),
            pltpu.VMEM(features.shape, bf16),
            pltpu.VMEM((256, SIDE, SIDE), bf16),
        ],
        in_specs=[SMEM] + [ANY] * (2 + len(FIRST)),
        out_specs=[VMEM] * 3,
        scratch_shapes=[pltpu.SemaphoreType.DMA((len(FIRST) + 2,))],
        compiler_params=PARAMS,
    )(
        where,
        *(stored(v) for v in (features, grad_out, own)),
        *(near(v) for v in (left, right, beside, own_other)),
    )
    low, high = pl.pallas_call(
        halves_kernel,
        out_shape=[pltpu.VMEM((8, SIDE, SIDE), bf16)] * 2,
        in_specs=[ANY] * 2,
        out_specs=[VMEM] * 2,
        scratch_shapes=[pltpu.SemaphoreType.DMA((2,))],
        compiler_params=PARAMS,
    )(near(left), near(right))
    second = [swap(left, "zl", 1), cross(right), swap(low, "x", 3), swap(high, "x", 1)]
    crossed = [swap(left, "core", 1)]
    second, crossed, whole, right, beside = lax.optimization_barrier(
        (second, crossed, whole, right, beside)
    )
    far = second[2:]
    beside_far = (swap(far[0], "zl", 1), cross(far[1]))
    both_far = jnp.concatenate(far, axis=0)
    crossed += [swap(piece, "core", 1) for piece in (right, beside, second[0])]
    whole = pl.pallas_call(
        more_kernel,
        out_shape=pltpu.VMEM((256, SIDE, SIDE), bf16),
        in_specs=[SMEM, VMEM] + [ANY] * len(MIDDLE),
        out_specs=VMEM,
        scratch_shapes=[pltpu.SemaphoreType.DMA((len(MIDDLE),))],
        input_output_aliases={1: 0},
        compiler_params=PARAMS,
    )(where, near(whole), *(near(piece) for piece in (*second, *crossed)))
    *beside_far, whole, both_far = lax.optimization_barrier((*beside_far, whole, both_far))
    crossed = [swap(piece, "core", 1) for piece in (second[1], *beside_far, both_far)]
    late = [near(piece) for piece in (*beside_far, *crossed)]
    slopes, whole = pl.pallas_call(
        forward_kernel,
        out_shape=[
            pltpu.VMEM((64, rows_here, SIDE), bf16),
            pltpu.VMEM((256, SIDE, SIDE), bf16),
        ],
        in_specs=[SMEM] * 3 + [VMEM] * 3 + [ANY] * len(LAST),
        out_specs=[VMEM, VMEM],
        scratch_shapes=[pltpu.SemaphoreType.DMA((len(LAST),))],
        input_output_aliases={5: 1},
        compiler_params=PARAMS,
    )(where, place, blocks, near(features_near), near(grad_near), near(whole), *late)
    slopes, others = lax.optimization_barrier((slopes, others))
    other_slopes = swap(slopes, "core", 1)
    xt = pl.pallas_call(
        transpose_kernel,
        out_shape=pltpu.VMEM((64, SIDE, 2 * rows_here), bf16),
        in_specs=[VMEM, VMEM],
        out_specs=VMEM,
        compiler_params=PARAMS,
    )(near(features_near), near(others))
    operands = (tile_row, tile_column, where, near(xt), near(slopes), near(other_slopes))
    sent = pl.pallas_call(
        functools.partial(partial_kernel, SENT, False),
        out_shape=[shape((16, SIDE, SIDE), bf16)] * 4,
        in_specs=[SMEM] * 3 + [VMEM] * 3,
        out_specs=[VMEM] * 4,
        compiler_params=PARAMS,
    )(*operands)
    got = [
        swap(value, axis, (1, 3)[half]) for value, (axis, half) in zip(sent, GROUPS, strict=True)
    ]
    kept = pl.pallas_call(
        functools.partial(partial_kernel, KEPT, True),
        out_shape=[shape((8, SIDE, SIDE), f32)] * 8,
        in_specs=[SMEM] * 3 + [VMEM] * 3,
        out_specs=[VMEM] * 8,
        compiler_params=PARAMS,
    )(*operands)
    kept = list(kept)
    after, kept[0] = lax.optimization_barrier((place, kept[0]))
    backward = functools.partial(
        pl.pallas_call,
        out_shape=shape(features.shape, bf16),
        out_specs=ANY,
        scratch_shapes=[
            pltpu.VMEM((32, rows_here, SIDE), bf16),
            pltpu.SemaphoreType.DMA((32,)),
        ],
        compiler_params=PARAMS,
    )
    grad_features = backward(
        functools.partial(backward_kernel, 0), in_specs=[SMEM] * 2 + [VMEM] * 3
    )(after, blocks, near(grad_near), near(whole), near(slopes))
    got, kept, grad_features = lax.optimization_barrier((got, kept, grad_features))
    second = [
        swap((kept[2 * i + 1] + got[i][8:].astype(f32)).astype(bf16), axis, (3, 1)[half])
        for i, (axis, half) in enumerate(GROUPS)
    ]
    held = [
        kept[2 * i] + got[i][:8].astype(f32) + second[i].astype(f32) for i in range(4)
    ]
    rest = [
        jnp.concatenate(
            [held[i].reshape(4, 2, SIDE, SIDE), held[i + 1].reshape(4, 2, SIDE, SIDE)], axis=1
        )
        for i in (0, 2)
    ]
    def reduce_last(parts, axis):
        away = [swap(parts[r].astype(bf16), axis, r).astype(f32) for r in (1, 2, 3)]
        return parts[0] + (away[0] + away[2]) + away[1]

    sums = [reduce_last(rest[0], "y")]
    sums[0], rest[1] = lax.optimization_barrier((sums[0], rest[1]))
    sums.append(reduce_last(rest[1], "x"))
    mine = (sums[1] + swap(sums[0], "zl", 1)).astype(bf16)
    place, mine = lax.optimization_barrier((place, mine))
    grad_features = backward(
        functools.partial(backward_kernel, 1),
        in_specs=[SMEM] * 2 + [VMEM] * 3 + [ANY],
        input_output_aliases={5: 0},
    )(place, blocks, near(grad_near), near(whole), near(slopes), grad_features)
    across = {r: swap(mine, "zh", r) for r in (1, 3, 2)}
    across = [across[r] for r in (1, 2, 3)]
    across, grad_features = lax.optimization_barrier((across, grad_features))
    group = pl.pallas_call(
        normalize_kernel,
        out_shape=shape((4, SIDE, SIDE), bf16),
        in_specs=[VMEM] * 4,
        out_specs=VMEM,
        compiler_params=PARAMS,
    )(mine, *across)
    spread = {r: swap(group, "y", r) for r in (1, 3, 2)}
    tile_update = pl.pallas_call(
        finish_kernel,
        out_shape=shape((16, SIDE, SIDE), f32),
        in_specs=[SMEM] + [VMEM] * 4,
        out_specs=VMEM,
        compiler_params=PARAMS,
    )(where, group, *(spread[r] for r in (1, 2, 3)))
    return grad_features, tile_update


def solution(mesh):
    grid = Mesh(mesh.devices.reshape(SIZES), AXES)
    return jax.shard_map(
        on_device,
        mesh=grid,
        in_specs=(P(AXES, None), P(AXES, None), P(("x", "zl", "core"), None, None), P(), P()),
        out_specs=(P(AXES, None), P(("x", "zl", "core"), None, None)),
        check_vma=False,
    )
```
